256 devices in a mesh: hx: 32 (over x, y, core), nb: 8 (over z).
Axes of the slice: x: 4, y: 4, z: 8, core: 2. Of those that a mesh axis runs over, the one named last changes fastest.
Arguments:
- partial_multipoles: bfloat16 [8, 16384, 1464], P('nb', 'hx'), may hold values from -6 to 6
- shared_slots: int32 [8, 16384], P('nb', 'hx'), may hold values from -1 to 1023, as said below
- m2l_sources: int32 [8, 2, 32768], P('nb', None, 'hx'), may hold values from 0 to 1023
- m2l_ops: bfloat16 [2, 1464, 1464], replicated, may hold values from -0.15625 to 0.15625
- positions: float32 [8, 3, 65536], P('nb', None, 'hx'), may hold values from -1 to 1
- forces: float32 [8, 3, 65536], P('nb', None, 'hx'), may hold values from -6 to 6
- leaf_counts: int32 [8, 512], P('nb', 'hx'), may hold values from 32 to 128
- neighbours: int32 [8, 8, 512], P('nb', None, 'hx'), may hold values from 0 to 47
Outputs:
- local_expansion: bfloat16 [8, 32768, 1464], P('nb', 'hx')
- velocity: float32 [8, 3, 65536], P('nb', None, 'hx')
The draws below stay inside these ranges and needn't reach their ends.
Inputs may be any that keep to these rules, and one draw needn't show every extreme that they name: `shared_slots`: rows j * 16 to (j + 1) * 16 - 1 of each device's 512 rows belong to owner j along hx. Each such block names exactly 4 distinct octants, each at least once; its other rows name one of these or are -1.
All inputs are finite; a program needn't handle non-finite values.
Results may differ from the reference program's by a relative error of at most 0.0048.
Values may be sent and summed in bfloat16 or wider, within the bound.
A program may use at most 64 MiB of HBM per device.

```python
import math
import jax
import jax.numpy as jnp
from jax import lax

K = 1464
NT = 2
OCT_DEV = 1024
ROWS_DEV = 512
LEAVES = 16
PTS = 128
NBR = 8
CAP = 16
UNIQ = 4
OCTANTS = 32768
ROWS = 16384
LEAF_ALL = 512
POINTS = 65536
N_HX = 32
N_NB = 8


def draw_shared_slots(key, part):
    slot_total = N_NB * N_HX * N_HX
    subkeys = jax.random.split(key, 4)
    chosen = jax.vmap(lambda subkey: jax.random.permutation(subkey, OCT_DEV)[:UNIQ])(jax.random.split(subkeys[0], slot_total))
    live_count = jax.random.randint(subkeys[1], (slot_total,), UNIQ, CAP + 1)
    position = jnp.arange(CAP, dtype=jnp.int32)[None, :]
    picks = jax.random.randint(subkeys[2], (slot_total, CAP), 0, UNIQ)
    picks = jnp.where(position < UNIQ, jnp.minimum(position, UNIQ - 1), picks)
    slot_ids = jnp.take_along_axis(chosen, picks, axis=1)
    slot_ids = jnp.where(position < live_count[:, None], slot_ids, -1)
    shuffle = jax.vmap(lambda subkey: jax.random.permutation(subkey, CAP))(jax.random.split(subkeys[3], slot_total))
    slot_ids = jnp.take_along_axis(slot_ids, shuffle, axis=1)
    return slot_ids.reshape(N_NB, N_HX * N_HX * CAP).astype(jnp.int32)


def place_ends(values, key, least, high):
    index_at = [jax.random.randint(jax.random.fold_in(key, axis), (), 0, length) for axis, length in enumerate(values.shape)]
    widest = values.shape.index(max(values.shape))
    next_to = index_at[:widest] + [(index_at[widest] + 1) % values.shape[widest]] + index_at[widest + 1:]
    return values.at[tuple(index_at)].set(least).at[tuple(next_to)].set(high)


def steps_of(own_key, dims, pieces, least, high):
    loudness, own = 1.0, jax.random.fold_in(own_key, 6)
    for axis_at, blocks in pieces:
        draws = jnp.exp(jax.random.uniform(jax.random.fold_in(own, axis_at), (blocks,), jnp.float32, least / len(pieces), high / len(pieces)))
        loudness = loudness * jnp.repeat(draws, dims[axis_at] // blocks).reshape([-1 if axis == axis_at else 1 for axis in range(len(dims))])
    return loudness


def bell_draw(own_key, dims, scale, limit, cuts=(), kind=jnp.bfloat16):
    loudness = steps_of(own_key, dims, cuts, -0.22, 0.18) if cuts else 1.0
    values = jax.random.normal(own_key, dims, jnp.float32) * scale * loudness
    return jnp.minimum(jnp.maximum(values, -limit), limit).astype(kind)


def setup_inputs(seed: int = 0) -> dict:
    arg_keys = jax.random.split(jax.random.key(seed), 9)
    return {
        "partial_multipoles": bell_draw(arg_keys[0], (N_NB, ROWS, K), 1.0, 6.0, ((0, 8), (1, 32))),
        "shared_slots": draw_shared_slots(jax.random.fold_in(arg_keys[8], 71), 0),
        "m2l_sources": place_ends(jax.random.randint(arg_keys[2], (N_NB, NT, OCTANTS), 0, OCT_DEV), jax.random.fold_in(arg_keys[2], 1), 0, OCT_DEV - 1).astype(jnp.int32),
        "m2l_ops": bell_draw(arg_keys[3], (NT, K, K), K ** -0.5, 0.15625),
        "positions": jnp.clip(jax.random.uniform(arg_keys[4], (N_NB, 3, POINTS), jnp.float32, -1.0, 1.0) * steps_of(arg_keys[4], (N_NB, 3, POINTS), ((0, 8), (2, 32)), -0.4, 0.0), -1.0, 1.0),
        "forces": bell_draw(arg_keys[5], (N_NB, 3, POINTS), 1.0, 6.0, ((0, 8), (2, 32)), jnp.float32),
        "leaf_counts": place_ends(jax.random.randint(arg_keys[6], (N_NB, LEAF_ALL), PTS // 4, PTS + 1), jax.random.fold_in(arg_keys[6], 1), PTS // 4, PTS).astype(jnp.int32),
        "neighbours": place_ends(jax.random.randint(arg_keys[7], (N_NB, NBR, LEAF_ALL), 0, 3 * LEAVES), jax.random.fold_in(arg_keys[7], 1), 0, (3 * LEAVES) - 1).astype(jnp.int32),
    }


reg_eps2 = 0.01
inv_eight_pi = 1.0 / (8.0 * math.pi)

def leaf_velocity(target_pos, target_live, source_pos, source_frc):
    offset = target_pos[:, None, :] - source_pos[:, :, None]
    dist_sq = lax.optimization_barrier(jnp.sum(offset * offset, axis=0)) + reg_eps2
    inverse_cube = 1.0 / (dist_sq * jnp.sqrt(dist_sq))
    projected = lax.optimization_barrier(jnp.sum(source_frc[:, :, None] * offset, axis=0))
    summand = (source_frc[:, :, None] * (dist_sq + reg_eps2)[None] + projected[None] * offset) * inverse_cube[None]
    return lax.optimization_barrier(jnp.sum(summand, axis=1)) * inv_eight_pi * target_live[None, :]

def leaves_block(own_pos, own_live, leaf_lists, source_table):

    def one_leaf(item):
        leaf_pos, leaf_live, leaf_list = item
        chosen = source_table[:, leaf_list, :].reshape(6, -1)
        return leaf_velocity(leaf_pos, leaf_live, chosen[:3], chosen[3:])
    result = lax.map(one_leaf, (own_pos.transpose(1, 0, 2), own_live, leaf_lists.T))
    return result.transpose(1, 0, 2)

def far_field(partial_multipoles, shared_slots, m2l_sources, m2l_ops):
    row_count = partial_multipoles.shape[1]
    octants = m2l_sources.shape[2]
    owner = jnp.arange(row_count, dtype=jnp.int32) % ROWS_DEV // CAP
    block_base = jnp.arange(octants, dtype=jnp.int32) // OCT_DEV * OCT_DEV

    def one_slab(index):
        slot_ids = shared_slots[index]
        shard_rows = partial_multipoles[index]
        target = jnp.where(slot_ids >= 0, owner * OCT_DEV + slot_ids, octants).astype(jnp.int32)
        sums = jax.ops.segment_sum(shard_rows.astype(jnp.float32), target, num_segments=octants + 1)[:octants]
        multipoles = sums.astype(jnp.bfloat16)
        total = jnp.zeros((octants, multipoles.shape[1]), jnp.float32)
        for direction in range(NT):
            picked = multipoles[block_base + m2l_sources[index, direction]]
            total = total + jnp.dot(picked, m2l_ops[direction], preferred_element_type=jnp.float32)
        return total.astype(jnp.bfloat16)
    return lax.map(one_slab, jnp.arange(N_NB, dtype=jnp.int32))

def near_field(positions, forces, leaf_counts, neighbours):
    leaf_all = leaf_counts.shape[1]
    per_leaf = positions.shape[2] // leaf_all
    live = (jnp.arange(per_leaf, dtype=jnp.int32)[None, None, :] < leaf_counts[:, :, None]).astype(jnp.float32)
    pos_four = positions.reshape(N_NB, 3, leaf_all, per_leaf)
    frc_four = forces.reshape(N_NB, 3, leaf_all, per_leaf) * live[:, None]
    packed = jnp.concatenate([pos_four, frc_four], axis=1)
    padded = jnp.pad(packed, ((1, 1), (0, 0), (0, 0), (0, 0)))

    def one_block(index):
        zero = jnp.zeros((), jnp.int32)
        slab = (index // N_HX).astype(jnp.int32)
        member = (index % N_HX).astype(jnp.int32)
        start = (member * LEAVES).astype(jnp.int32)
        window = lax.dynamic_slice(padded, (slab, zero, start, zero), (3, 6, LEAVES, per_leaf))
        source_table = window.transpose(1, 0, 2, 3).reshape(6, 3 * LEAVES, per_leaf)
        own_pos = lax.dynamic_slice(pos_four, (slab, zero, start, zero), (1, 3, LEAVES, per_leaf))[0]
        own_live = lax.dynamic_slice(live, (slab, start, zero), (1, LEAVES, per_leaf))[0]
        leaf_lists = lax.dynamic_slice(neighbours, (slab, zero, start), (1, NBR, LEAVES))[0]
        return leaves_block(own_pos, own_live, leaf_lists, source_table)
    result = lax.map(one_block, jnp.arange(N_NB * N_HX, dtype=jnp.int32))
    result = result.reshape(N_NB, N_HX, 3, LEAVES, per_leaf).transpose(0, 2, 1, 3, 4)
    return result.reshape(N_NB, 3, leaf_all * per_leaf)

def reference(partial_multipoles, shared_slots, m2l_sources, m2l_ops, positions, forces, leaf_counts, neighbours):
    local_expansion = far_field(partial_multipoles, shared_slots, m2l_sources, m2l_ops)
    velocity = near_field(positions, forces, leaf_counts, neighbours)
    return (local_expansion, velocity)
```

```python
import functools
import math

import jax
import jax.numpy as jnp
from jax import lax
from jax.experimental import pallas as pl
from jax.experimental.pallas import tpu as pltpu
from jax.sharding import PartitionSpec as P

EPS = 0.01
SCALE = 1.0 / (8.0 * math.pi)
MESH = pl.DeviceIdType.MESH
UNIQ = 4
CAP = 16
FEAT = 48
f32 = jnp.float32
bf16 = jnp.bfloat16
NT_DIMS = (((1,), (1,)), ((), ()))


def rounded(v):
    return v.astype(bf16).astype(f32)


def split3(v):
    a = rounded(v)
    b = rounded(v - a)
    return a, b, rounded(v - a - b)


def rank_keys(slots):
    lane = lax.broadcasted_iota(jnp.int32, slots.shape, 1)
    group = lax.broadcasted_iota(jnp.int32, slots.shape, 0)
    place = lane & (CAP - 1)
    dup = jnp.zeros(slots.shape, jnp.int32)
    for s in range(1, CAP):
        same = (pltpu.roll(slots, s, 1) == slots) & (place >= s)
        dup = jnp.where(same, 1, dup)
    first = (dup == 0) & (slots >= 0)
    named = jnp.where(first, slots, 1 << 20)
    rank = jnp.zeros(slots.shape, jnp.int32)
    for s in range(1, CAP):
        below = (pltpu.roll(named, s, 1) < slots) & (place >= s)
        rank = rank + jnp.where(below, 1, 0)
        below = (pltpu.roll(named, 128 - s, 1) < slots) & (place < CAP - s)
        rank = rank + jnp.where(below, 1, 0)
    key = jnp.where(slots >= 0, group * (128 // CAP * UNIQ) + (lane >> 4) * UNIQ + rank, -1)
    return key, first


def exchange_kernel(
    n_hx, n_nb, slots_ref, pos_ref, frc_ref, counts_ref, nbr_ref, rows_hbm, ops_hbm,
    prod_ref, ids_ref, vel_ref,
    rows, ops, send, recv, gathered, raw, ysrc, ylow, xtgt,
    send_sem, recv_sem, halo_send, halo_recv, rows_sem, ops_sem,
):
    hx, nb = lax.axis_index("hx"), lax.axis_index("nb")
    after, before = lax.rem(nb + 1, n_nb), lax.rem(nb + n_nb - 1, n_nb)
    coeffs = rows_hbm.shape[0]
    leaves, lanes = pos_ref.shape[1], pos_ref.shape[2]

    barrier = pltpu.get_barrier_semaphore()

    def greet(d, c):
        pl.semaphore_signal(barrier, inc=1, device_id={"hx": lax.rem(hx + d, n_hx)}, device_id_type=MESH)
        return c

    lax.fori_loop(1, n_hx, greet, 0)
    for other in (after, before):
        pl.semaphore_signal(barrier, inc=1, device_id={"nb": other}, device_id_type=MESH)

    rows_copy = pltpu.make_async_copy(rows_hbm, rows.at[pl.ds(0, coeffs), :], rows_sem)
    rows_copy.start()
    ops_copies = [pltpu.make_async_copy(ops_hbm.at[t], ops.at[t], ops_sem.at[t]) for t in range(ops.shape[0])]

    lane_ids = lax.broadcasted_iota(jnp.int32, (1, lanes), 1)
    for l in range(leaves):
        live = jnp.where(lane_ids < counts_ref[0, l], 1.0, 0.0).astype(f32)
        block = [pos_ref[c, l : l + 1, :] for c in range(3)]
        block += [frc_ref[c, l : l + 1, :] * live for c in range(3)]
        block += [jnp.ones((1, lanes), f32), jnp.zeros((1, lanes), f32)]
        raw[1, l] = jnp.concatenate(block, axis=0)

    slots = slots_ref[...]
    four = [slots[:, g * lanes : (g + 1) * lanes] for g in range(4)]
    slots8 = jnp.concatenate(four + four, axis=0)
    key, first = rank_keys(slots8)
    n_keys = n_hx * UNIQ
    key_ids = lax.broadcasted_iota(jnp.int32, (n_keys, lanes), 0)
    pick = jnp.concatenate(
        [jnp.where(key_ids == key[g : g + 1, :], 1.0, 0.0).astype(bf16) for g in range(4)], axis=1
    )
    high = jnp.where(first, slots8 >> 5, 0).astype(f32)
    low = jnp.where(first, slots8 & 31, 0).astype(f32)
    zero6 = jnp.zeros((6, lanes), f32)
    marks = jnp.concatenate(
        [jnp.concatenate([high[g : g + 1], low[g : g + 1], zero6], axis=0) for g in range(4)], axis=1
    )
    rows[coeffs : coeffs + 8, :] = marks.astype(bf16)
    rows_copy.wait()
    for c in ops_copies:
        c.start()
    sums = lax.dot_general(pick, rows[...], NT_DIMS, preferred_element_type=f32)
    for j in range(n_hx):
        send[j] = sums[j * UNIQ : (j + 1) * UNIQ, :].astype(bf16)

    pl.semaphore_wait(barrier, n_hx - 1 + 2)

    def halo(k, target):
        return pltpu.make_async_remote_copy(
            src_ref=raw.at[1], dst_ref=raw.at[k], send_sem=halo_send.at[k // 2], recv_sem=halo_recv.at[k // 2],
            device_id={"nb": target}, device_id_type=MESH,
        )

    up, down = halo(0, after), halo(2, before)
    up.start()
    down.start()

    def chunk(d):
        target = lax.rem(hx + d, n_hx)
        return pltpu.make_async_remote_copy(
            src_ref=send.at[target], dst_ref=recv.at[hx], send_sem=send_sem.at[d], recv_sem=recv_sem.at[d],
            device_id={"hx": target}, device_id_type=MESH,
        )

    def start(d, c):
        chunk(d).start()
        return c

    lax.fori_loop(1, n_hx, start, 0)
    recv[hx] = send[hx]

    row8 = lax.broadcasted_iota(jnp.int32, (leaves, 8, lanes), 1)
    own = raw[1]
    own_high = rounded(own)
    own_low = rounded(own - own_high)
    x_high, x_low = jnp.where(row8 < 3, own_high, 0.0), jnp.where(row8 < 3, own_low, 0.0)
    x_sum = x_high + x_low
    t1, t2, t3 = split3(jnp.sum(x_sum * x_sum, axis=1, keepdims=True) + EPS)
    is6 = row8 == 6
    zero8 = jnp.zeros((leaves, 8, lanes), f32)
    q_side = [
        jnp.where(is6, t1, -2.0 * x_high), -2.0 * x_high, jnp.where(is6, t2, -2.0 * x_low), -2.0 * x_low,
        jnp.where(is6, t3, jnp.where(row8 < 3, 1.0, 0.0)), zero8,
    ]
    force_rows = (row8 >= 3) & (row8 < 6)
    p_high, p_low = pltpu.roll(x_high, 3, 1), pltpu.roll(x_low, 3, 1)
    p_side = [p_high, p_high, p_low, p_low, jnp.where(force_rows, -1.0, 0.0), zero8]
    xtgt[:, :, :lanes] = jnp.concatenate(q_side, axis=1).astype(bf16)
    xtgt[:, :, lanes:] = jnp.concatenate(p_side, axis=1).astype(bf16)

    def source_side(k, mask):
        src = raw[k]
        if mask is not None:
            src = jnp.where(force_rows, src * mask, src)
        s_high = rounded(src)
        s_low = rounded(src - s_high)
        s_sum = s_high + s_low
        s_pos = jnp.where(row8 < 3, s_sum, 0.0)
        y1, y2, y3 = split3(jnp.sum(s_pos * s_pos, axis=1, keepdims=True))
        g1, g2, g3 = split3(jnp.sum(s_pos * pltpu.roll(s_sum, 5, 1), axis=1, keepdims=True))
        extra = zero8
        for at, v in enumerate((y1, y2, y3, g1, g2, g3, jnp.ones_like(y1))):
            extra = jnp.where(row8 == at, v, extra)
        table = jnp.concatenate([s_high, s_low, s_high, s_low, extra, zero8], axis=1)
        at = pl.ds(k * leaves, leaves)
        ysrc[at] = jnp.swapaxes(table, 1, 2).astype(bf16)
        ylow[at] = jnp.concatenate([s_high, s_low], axis=1).astype(bf16)

    source_side(1, None)
    up.wait_recv()
    source_side(0, jnp.where(nb > 0, 1.0, 0.0).astype(f32))
    down.wait_recv()
    source_side(2, jnp.where(nb < n_nb - 1, 1.0, 0.0).astype(f32))

    def leaf(i, c):
        x = xtgt[i]
        total = jnp.zeros((16, 2 * lanes), f32)
        for pair in range(nbr_ref.shape[0] // 2):
            kernels, weights = [], []
            for n in (2 * pair, 2 * pair + 1):
                which = nbr_ref[n, i]
                qp = jnp.dot(ysrc[which], x, preferred_element_type=f32)
                r = lax.rsqrt(qp[:, :lanes])
                w = r * r * r
                kernels.append(jnp.concatenate([r + EPS * w, qp[:, lanes:] * w], axis=1).astype(bf16))
                weights.append(ylow[which])
            total = total + jnp.dot(
                jnp.concatenate(weights, axis=1), jnp.concatenate(kernels, axis=0), preferred_element_type=f32
            )
        both = total[:8] + total[8:]
        first_part, second_part = both[:, :lanes], both[:, lanes:]
        x_own = raw[1, i]
        live = jnp.where(lane_ids < counts_ref[0, i], SCALE, 0.0).astype(f32)
        u = pltpu.roll(first_part, 5, 0) + x_own * second_part[6:7, :] - second_part
        vel_ref[i] = u * live
        return c

    lax.fori_loop(0, leaves, leaf, 0)

    def finish(d, c):
        chunk(d).wait_recv()
        return c

    lax.fori_loop(1, n_hx, finish, 0)
    for j in range(n_hx // 4):
        four = [recv[4 * j + k].astype(f32) for k in range(4)]
        gathered[16 * j : 16 * (j + 1), :] = jnp.concatenate(four, axis=0).astype(bf16)
    whose = gathered[:, coeffs : coeffs + 2].astype(f32)
    ids_ref[...] = jnp.broadcast_to((whose[:, 0:1] * 32.0 + whose[:, 1:2]).astype(jnp.int32), ids_ref.shape)
    for t, c in enumerate(ops_copies):
        c.wait()
        part = jnp.dot(gathered[:, :coeffs], ops[t], preferred_element_type=f32)
        prod_ref[t * n_keys : (t + 1) * n_keys, :] = part.astype(bf16)

    def sent(d, c):
        chunk(d).wait_send()
        return c

    lax.fori_loop(1, n_hx, sent, 0)
    up.wait_send()
    down.wait_send()


def select_kernel(ids_ref, src_ref, prod_ref, vel_in, out_ref, vel_out, prod_t):
    @pl.when(pl.program_id(0) == 0)
    def _():
        prod_t[...] = prod_ref[...].astype(f32).T.astype(bf16)
        v = vel_in[...]
        for c in range(3):
            vel_out[c] = v[:, c, :]

    ids = ids_ref[:, 0:1]
    pick = jnp.concatenate(
        [jnp.where(ids == src_ref[t : t + 1, :], 1.0, 0.0).astype(bf16) for t in range(src_ref.shape[0])], axis=0
    )
    out_ref[...] = jnp.dot(prod_t[...], pick, preferred_element_type=f32).astype(bf16)


def on_device(
    n_hx, n_nb, partial_multipoles, shared_slots, m2l_sources, m2l_ops, positions, forces, leaf_counts, neighbours
):
    rows_t = partial_multipoles[0].T
    coeffs, n_rows = rows_t.shape
    n_dirs, owned = m2l_sources.shape[1:]
    leaves = leaf_counts.shape[1]
    lanes = positions.shape[2] // leaves
    n_keys = n_hx * UNIQ
    vmem = pl.BlockSpec(memory_space=pltpu.VMEM)
    smem = pl.BlockSpec(memory_space=pltpu.SMEM)
    hbm = pl.BlockSpec(memory_space=pl.ANY)
    width = coeffs + 8
    prod, ids, vel = pl.pallas_call(
        functools.partial(exchange_kernel, n_hx, n_nb),
        out_shape=(
            jax.ShapeDtypeStruct((n_dirs * n_keys, coeffs), bf16),
            jax.ShapeDtypeStruct((n_keys, 128), jnp.int32),
            jax.ShapeDtypeStruct((leaves, 8, lanes), f32),
        ),
        in_specs=[vmem, vmem, vmem, smem, smem, hbm, hbm],
        out_specs=(vmem, vmem, vmem),
        scratch_shapes=[
            pltpu.VMEM((width, n_rows), bf16),
            pltpu.VMEM((n_dirs, coeffs, coeffs), bf16),
            pltpu.VMEM((n_hx, UNIQ, width), bf16),
            pltpu.VMEM((n_hx, UNIQ, width), bf16),
            pltpu.VMEM((n_keys, width), bf16),
            pltpu.VMEM((3, leaves, 8, lanes), f32),
            pltpu.VMEM((3 * leaves, lanes, FEAT), bf16),
            pltpu.VMEM((3 * leaves, 16, lanes), bf16),
            pltpu.VMEM((leaves, FEAT, 2 * lanes), bf16),
            pltpu.SemaphoreType.DMA((n_hx,)),
            pltpu.SemaphoreType.DMA((n_hx,)),
            pltpu.SemaphoreType.DMA((2,)),
            pltpu.SemaphoreType.DMA((2,)),
            pltpu.SemaphoreType.DMA,
            pltpu.SemaphoreType.DMA((n_dirs,)),
        ],
        compiler_params=pltpu.CompilerParams(
            collective_id=0, has_side_effects=True, vmem_limit_bytes=48 * 1024 * 1024
        ),
        name="exchange",
    )(
        shared_slots, positions.reshape(3, leaves, lanes), forces.reshape(3, leaves, lanes), leaf_counts,
        neighbours[0], rows_t, m2l_ops,
    )
    tile = 256
    out_t, velocity = pl.pallas_call(
        select_kernel,
        grid=(owned // tile,),
        out_shape=(
            jax.ShapeDtypeStruct((coeffs, owned), bf16),
            jax.ShapeDtypeStruct((3, leaves, lanes), f32),
        ),
        in_specs=[
            pl.BlockSpec((n_keys, 128), lambda i: (0, 0)),
            pl.BlockSpec((n_dirs, tile), lambda i: (0, i)),
            pl.BlockSpec((n_dirs * n_keys, coeffs), lambda i: (0, 0)),
            pl.BlockSpec((leaves, 8, lanes), lambda i: (0, 0, 0)),
        ],
        out_specs=(
            pl.BlockSpec((coeffs, tile), lambda i: (0, i)),
            pl.BlockSpec((3, leaves, lanes), lambda i: (0, 0, 0)),
        ),
        scratch_shapes=[pltpu.VMEM((coeffs, n_dirs * n_keys), bf16)],
        compiler_params=pltpu.CompilerParams(dimension_semantics=("arbitrary",)),
        name="select",
    )(ids, m2l_sources[0], prod, vel)
    return out_t.T[None], velocity.reshape(1, 3, leaves * lanes)


def solution(mesh):
    placed = (
        P("nb", "hx", None),
        P("nb", "hx"),
        P("nb", None, "hx"),
        P(),
        P("nb", None, "hx"),
        P("nb", None, "hx"),
        P("nb", "hx"),
        P("nb", None, "hx"),
    )
    return jax.shard_map(
        functools.partial(on_device, mesh.shape["hx"], mesh.shape["nb"]),
        mesh=mesh,
        in_specs=placed,
        out_specs=(P("nb", "hx", None), P("nb", None, "hx")),
        check_vma=False,
    )
```

```python
import functools
import math

import jax
import jax.numpy as jnp
from jax import lax
from jax.experimental import pallas as pl
from jax.experimental.pallas import tpu as pltpu
from jax.sharding import PartitionSpec as P

EPS = 0.01
SCALE = 1.0 / (8.0 * math.pi)
MESH = pl.DeviceIdType.MESH
UNIQ = 4
CAP = 16
QROWS = 32
FROWS = 48
f32 = jnp.float32
bf16 = jnp.bfloat16
NT_DIMS = (((1,), (1,)), ((), ()))


def rounded(v):
    return v.astype(bf16).astype(f32)


def split3(v):
    a = rounded(v)
    b = rounded(v - a)
    return a, b, rounded(v - a - b)


def rank_keys(slots):
    lane = lax.broadcasted_iota(jnp.int32, slots.shape, 1)
    group = lax.broadcasted_iota(jnp.int32, slots.shape, 0)
    place = lane & (CAP - 1)
    dup = jnp.zeros(slots.shape, jnp.int32)
    for s in range(1, CAP):
        same = (pltpu.roll(slots, s, 1) == slots) & (place >= s)
        dup = jnp.where(same, 1, dup)
    first = (dup == 0) & (slots >= 0)
    named = jnp.where(first, slots, 1 << 20)
    rank = jnp.zeros(slots.shape, jnp.int32)
    for s in range(1, CAP):
        below = (pltpu.roll(named, s, 1) < slots) & (place >= s)
        rank = rank + jnp.where(below, 1, 0)
        below = (pltpu.roll(named, 128 - s, 1) < slots) & (place < CAP - s)
        rank = rank + jnp.where(below, 1, 0)
    key = jnp.where(slots >= 0, group * (128 // CAP * UNIQ) + (lane >> 4) * UNIQ + rank, -1)
    return key, first


def exchange_kernel(
    n_hx, n_nb, slots_hbm, pos_hbm, frc_hbm, counts_hbm, nbr_hbm, src_hbm, rows_hbm, ops_hbm,
    prod_ref, pick_ref, vel_ref,
    slots_ref, pos_ref, frc_ref, counts_ref, nbr_ref, src_ref,
    rows, ops, send, recv, gathered, raw, alive, yq, feat, xtgt, moments,
    send_sem, recv_sem, halo_send, halo_recv, small_sem, rows_sem, ops_sem,
):
    hx, nb = lax.axis_index("hx"), lax.axis_index("nb")
    after, before = lax.rem(nb + 1, n_nb), lax.rem(nb + n_nb - 1, n_nb)
    coeffs = rows_hbm.shape[0]
    leaves, lanes = pos_ref.shape[1], pos_ref.shape[2]
    half = send.shape[2]
    n_keys = n_hx * UNIQ

    small = [
        pltpu.make_async_copy(a, b, small_sem.at[k])
        for k, (a, b) in enumerate(
            (
                (slots_hbm, slots_ref), (counts_hbm, counts_ref), (pos_hbm, pos_ref), (frc_hbm, frc_ref),
                (nbr_hbm, nbr_ref), (src_hbm, src_ref),
            )
        )
    ]
    for c in small[:4]:
        c.start()
    rows_copy = pltpu.make_async_copy(rows_hbm, rows.at[pl.ds(0, coeffs), :], rows_sem)
    rows_copy.start()
    for c in small[4:]:
        c.start()

    barrier = pltpu.get_barrier_semaphore()
    for d in range(1, n_hx):
        pl.semaphore_signal(barrier, inc=1, device_id={"hx": lax.rem(hx + d, n_hx)}, device_id_type=MESH)
    for other in (after, before):
        pl.semaphore_signal(barrier, inc=1, device_id={"nb": other}, device_id_type=MESH)

    ops_copies = [pltpu.make_async_copy(ops_hbm.at[t], ops.at[t], ops_sem.at[t]) for t in range(ops.shape[0])]

    small[0].wait()
    slots = slots_ref[...]
    four = [slots[:, g * lanes : (g + 1) * lanes] for g in range(4)]
    slots8 = jnp.concatenate(four + four, axis=0)
    key, first = rank_keys(slots8)
    key_ids = lax.broadcasted_iota(jnp.int32, (n_keys, lanes), 0)
    choose = jnp.concatenate(
        [jnp.where(key_ids == key[g : g + 1, :], 1.0, 0.0).astype(bf16) for g in range(4)], axis=1
    )
    high = jnp.where(first, slots8 >> 5, 0).astype(f32)
    low = jnp.where(first, slots8 & 31, 0).astype(f32)
    zero6 = jnp.zeros((6, lanes), f32)
    marks = jnp.concatenate(
        [jnp.concatenate([high[g : g + 1], low[g : g + 1], zero6], axis=0) for g in range(4)], axis=1
    )
    rows[coeffs : coeffs + 8, :] = marks.astype(bf16)
    rows[coeffs + 8 :, :] = jnp.zeros((rows.shape[0] - coeffs - 8, rows.shape[1]), bf16)

    for c in small[1:4]:
        c.wait()
    lane_ids = lax.broadcasted_iota(jnp.int32, (1, lanes), 1)
    for l in range(leaves):
        live = jnp.where(lane_ids < counts_ref[0, l], 1.0, 0.0).astype(f32)
        alive[l : l + 1, :] = live
        block = [pos_ref[c, l : l + 1, :] for c in range(3)]
        block += [frc_ref[c, l : l + 1, :] * live for c in range(3)]
        block += [jnp.ones((1, lanes), f32), jnp.zeros((1, lanes), f32)]
        raw[1, l] = jnp.concatenate(block, axis=0)

    rows_copy.wait()
    for c in ops_copies:
        c.start()
    sums = lax.dot_general(choose, rows[...], NT_DIMS, preferred_element_type=f32)
    upper = lax.broadcasted_iota(jnp.int32, (8, half), 0) < UNIQ
    for v in range(n_hx // 2):
        left, right = sums[8 * v : 8 * v + 8, :half], sums[8 * v : 8 * v + 8, half:]
        send[2 * v] = jnp.where(upper, left, pltpu.roll(right, UNIQ, 0)).astype(bf16)
        send[2 * v + 1] = jnp.where(upper, pltpu.roll(left, UNIQ, 0), right).astype(bf16)

    pl.semaphore_wait(barrier, n_hx - 1 + 2)

    def halo(k, target):
        return pltpu.make_async_remote_copy(
            src_ref=raw.at[1], dst_ref=raw.at[k], send_sem=halo_send.at[k // 2], recv_sem=halo_recv.at[k // 2],
            device_id={"nb": target}, device_id_type=MESH,
        )

    up, down = halo(0, after), halo(2, before)
    up.start()
    down.start()

    def chunk(d):
        target = lax.rem(hx + d, n_hx)
        return pltpu.make_async_remote_copy(
            src_ref=send.at[target], dst_ref=recv.at[hx], send_sem=send_sem.at[d], recv_sem=recv_sem.at[d],
            device_id={"hx": target}, device_id_type=MESH,
        )

    chunks = [chunk(d) for d in range(1, n_hx)]
    for c in chunks:
        c.start()
    recv[hx] = send[hx]

    row8 = lax.broadcasted_iota(jnp.int32, (leaves, 8, lanes), 1)
    zero8 = jnp.zeros((leaves, 8, lanes), f32)
    is_pos, is_frc = row8 < 3, (row8 >= 3) & (row8 < 6)

    def pos_sum(v):
        return jnp.sum(jnp.where(is_pos, v, 0.0), axis=1, keepdims=True)

    own = raw[1]
    own_high = rounded(own)
    own_low = rounded(own - own_high)
    x_sum = own_high + own_low
    t1, t2, t3 = split3(pos_sum(x_sum * x_sum) + EPS)
    two_high, two_low = -2.0 * own_high, -2.0 * own_low
    x_table = jnp.concatenate(
        [
            jnp.where(is_pos, two_high, jnp.where(is_frc, pltpu.roll(two_high, 3, 1), jnp.where(row8 == 6, t1, t2))),
            jnp.where(is_pos, two_low, jnp.where(is_frc, pltpu.roll(two_low, 3, 1), jnp.where(row8 == 6, t3, 0.0))),
            jnp.where(is_pos, 1.0, zero8),
            zero8,
        ],
        axis=1,
    )
    xtgt[...] = jnp.swapaxes(x_table, 1, 2).astype(bf16)

    def source_side(k, mask):
        src = raw[k]
        if mask is not None:
            src = jnp.where(is_frc, src * mask, src)
        at = pl.ds(k * leaves, leaves)
        s_high = rounded(src)
        s_low = rounded(src - s_high)
        s_sum = s_high + s_low
        y1, y2, y3 = split3(pos_sum(s_sum * s_sum))
        pairs = jnp.where(is_pos, s_high, jnp.where(is_frc, pltpu.roll(s_low, 3, 1), 1.0))
        squares = jnp.where(row8 == 0, y1, jnp.where(row8 == 1, y2, jnp.where(row8 == 2, y3, 0.0)))
        yq[at] = jnp.concatenate([pairs, pairs, squares, zero8], axis=1).astype(bf16)
        square = pos_sum(src * src)
        f_at0, f_at6 = pltpu.roll(src, 5, 1), pltpu.roll(src, 3, 1)
        f_dot_y = pos_sum(src * f_at0)
        z = src[:, 2:3, :]
        products = jnp.where(is_pos, f_at0, jnp.where(is_frc, src, f_at6)) * jnp.where(
            is_pos, src[:, 0:1, :], jnp.where(is_frc, src[:, 1:2, :], z)
        )
        second = pltpu.roll(src, 1, 1) * square + pltpu.roll(src, 4, 1) * f_dot_y
        others = jnp.where(
            row8 == 0, f_at6 * z, jnp.where(row8 < 4, pltpu.roll(src, 6, 1), jnp.where(row8 < 7, second, 0.0))
        )
        a, b = split3(products), split3(others)
        feat[at] = jnp.concatenate([a[0], b[0], a[1], b[1], a[2], b[2]], axis=1).astype(bf16)

    source_side(1, None)
    up.wait_recv()
    source_side(0, jnp.where(nb > 0, 1.0, 0.0).astype(f32))
    down.wait_recv()
    source_side(2, jnp.where(nb < n_nb - 1, 1.0, 0.0).astype(f32))
    small[4].wait()

    def leaf(i, c):
        which = [nbr_ref[n, i] for n in range(nbr_ref.shape[0])]
        q = jnp.dot(xtgt[i], jnp.concatenate([yq[n] for n in which], axis=1), preferred_element_type=f32)
        r = lax.rsqrt(q)
        w = (r * r * r).astype(bf16)
        m = lax.dot_general(
            jnp.concatenate([feat[n] for n in which], axis=1), w, NT_DIMS, preferred_element_type=f32
        )
        moments[i] = m[:16] + m[16:32] + m[32:]
        return c

    lax.fori_loop(0, leaves, leaf, 0, unroll=True)
    m = [moments[:, k, :] for k in range(15)]
    x = [pos_ref[c] for c in range(3)]
    two_e = x[0] * x[0] + x[1] * x[1] + x[2] * x[2] + 2.0 * EPS
    along = x[0] * m[9] + x[1] * m[10] + x[2] * m[11] - (m[0] + m[4] + m[8])
    live = alive[...] * SCALE
    for c in range(3):
        u = two_e * m[9 + c] + x[c] * along + m[12 + c]
        for b in range(3):
            u = u - x[b] * (2.0 * m[3 * b + c] + m[3 * c + b])
        vel_ref[c] = u * live

    for c in chunks:
        c.wait_recv()
    for v in range(n_hx // 4):
        lefts, rights = [], []
        for k in (4 * v, 4 * v + 2):
            a, b = recv[k].astype(f32), recv[k + 1].astype(f32)
            lefts.append(jnp.where(upper, a, pltpu.roll(b, UNIQ, 0)))
            rights.append(jnp.where(upper, pltpu.roll(a, UNIQ, 0), b))
        gathered[16 * v : 16 * (v + 1), :half] = jnp.concatenate(lefts, axis=0).astype(bf16)
        gathered[16 * v : 16 * (v + 1), half:] = jnp.concatenate(rights, axis=0).astype(bf16)
    whose = gathered[:, coeffs : coeffs + 2].astype(f32)
    ids = (whose[:, 0:1] * 32.0 + whose[:, 1:2]).astype(jnp.int32)
    small[5].wait()
    for t, c in enumerate(ops_copies):
        c.wait()
        part = jnp.dot(gathered[:, :coeffs], ops[t], preferred_element_type=f32)
        prod_ref[:, t * n_keys : (t + 1) * n_keys] = part.T.astype(bf16)
        pick_ref[t * n_keys : (t + 1) * n_keys, :] = jnp.where(ids == src_ref[t : t + 1, :], 1.0, 0.0).astype(bf16)

    for c in chunks:
        c.wait_send()
    up.wait_send()
    down.wait_send()


def select_kernel(prod_ref, pick_ref, vel_in, out_ref, vel_out):
    @pl.when(pl.program_id(0) == 0)
    def _():
        vel_out[...] = vel_in[...]

    at = pl.ds(pl.multiple_of(pl.program_id(0) * out_ref.shape[1], 128), out_ref.shape[1])
    out_ref[...] = jnp.dot(prod_ref[...], pick_ref[:, at], preferred_element_type=f32).astype(bf16)


def on_device(
    n_hx, n_nb, partial_multipoles, shared_slots, m2l_sources, m2l_ops, positions, forces, leaf_counts, neighbours
):
    rows_t = partial_multipoles[0].T
    coeffs, n_rows = rows_t.shape
    n_dirs, owned = m2l_sources.shape[1:]
    n_near = neighbours.shape[1]
    leaves = leaf_counts.shape[1]
    lanes = positions.shape[2] // leaves
    n_keys = n_hx * UNIQ
    vmem = pl.BlockSpec(memory_space=pltpu.VMEM)
    hbm = pl.BlockSpec(memory_space=pltpu.HBM)
    half = pl.cdiv(coeffs + 8, 256) * 128
    i32 = jnp.int32
    prod, pick, vel = pl.pallas_call(
        functools.partial(exchange_kernel, n_hx, n_nb),
        out_shape=(
            jax.ShapeDtypeStruct((coeffs, n_dirs * n_keys), bf16),
            jax.ShapeDtypeStruct((n_dirs * n_keys, owned), bf16),
            jax.ShapeDtypeStruct((3, leaves, lanes), f32),
        ),
        in_specs=[hbm] * 8,
        out_specs=(vmem, vmem, vmem),
        scratch_shapes=[
            pltpu.VMEM((1, n_rows), i32),
            pltpu.VMEM((3, leaves, lanes), f32),
            pltpu.VMEM((3, leaves, lanes), f32),
            pltpu.SMEM((1, leaves), i32),
            pltpu.SMEM((n_near, leaves), i32),
            pltpu.VMEM((n_dirs, owned), i32),
            pltpu.VMEM((2 * half, n_rows), bf16),
            pltpu.VMEM((n_dirs, coeffs, coeffs), bf16),
            pltpu.VMEM((n_hx, 2 * UNIQ, half), bf16),
            pltpu.VMEM((n_hx, 2 * UNIQ, half), bf16),
            pltpu.VMEM((n_keys, 2 * half), bf16),
            pltpu.VMEM((3, leaves, 8, lanes), f32),
            pltpu.VMEM((leaves, lanes), f32),
            pltpu.VMEM((3 * leaves, QROWS, lanes), bf16),
            pltpu.VMEM((3 * leaves, FROWS, lanes), bf16),
            pltpu.VMEM((leaves, lanes, QROWS), bf16),
            pltpu.VMEM((leaves, 16, lanes), f32),
            pltpu.SemaphoreType.DMA((n_hx,)),
            pltpu.SemaphoreType.DMA((n_hx,)),
            pltpu.SemaphoreType.DMA((2,)),
            pltpu.SemaphoreType.DMA((2,)),
            pltpu.SemaphoreType.DMA((6,)),
            pltpu.SemaphoreType.DMA,
            pltpu.SemaphoreType.DMA((n_dirs,)),
        ],
        compiler_params=pltpu.CompilerParams(
            collective_id=0, has_side_effects=True, vmem_limit_bytes=48 * 1024 * 1024
        ),
        name="exchange",
    )(
        *[
            pltpu.with_memory_space_constraint(v, pltpu.HBM)
            for v in (
                shared_slots, positions.reshape(3, leaves, lanes), forces.reshape(3, leaves, lanes), leaf_counts,
                neighbours[0], m2l_sources[0], rows_t, m2l_ops,
            )
        ]
    )
    tile = 256
    out_t, velocity = pl.pallas_call(
        select_kernel,
        grid=(owned // tile,),
        out_shape=(
            jax.ShapeDtypeStruct((coeffs, owned), bf16),
            jax.ShapeDtypeStruct((3, leaves, lanes), f32),
        ),
        in_specs=[vmem, vmem, vmem],
        out_specs=(
            pl.BlockSpec((coeffs, tile), lambda i: (0, i)),
            pl.BlockSpec((3, leaves, lanes), lambda i: (0, 0, 0)),
        ),
        compiler_params=pltpu.CompilerParams(dimension_semantics=("arbitrary",), vmem_limit_bytes=16 * 1024 * 1024),
        name="select",
    )(prod, pick, vel)
    return out_t.T[None], velocity.reshape(1, 3, leaves * lanes)


def solution(mesh):
    placed = (
        P("nb", "hx", None),
        P("nb", "hx"),
        P("nb", None, "hx"),
        P(),
        P("nb", None, "hx"),
        P("nb", None, "hx"),
        P("nb", "hx"),
        P("nb", None, "hx"),
    )
    return jax.shard_map(
        functools.partial(on_device, mesh.shape["hx"], mesh.shape["nb"]),
        mesh=mesh,
        in_specs=placed,
        out_specs=(P("nb", "hx", None), P("nb", None, "hx")),
        check_vma=False,
    )
```

```python
import functools
import math

import jax
import jax.numpy as jnp
from jax import lax
from jax.experimental import pallas as pl
from jax.experimental.pallas import tpu as pltpu
from jax.sharding import PartitionSpec as P

EPS = 0.01
SCALE = 1.0 / (8.0 * math.pi)
MESH = pl.DeviceIdType.MESH
UNIQ = 4
CAP = 16
QROWS = 32
FROWS = 48
f32 = jnp.float32
bf16 = jnp.bfloat16
NT_DIMS = (((1,), (1,)), ((), ()))


def peer_steps(n_hx):
    side = math.isqrt(n_hx // 2)
    steps = [(dx, dy, dc) for dx in range(side) for dy in range(side) for dc in range(2) if dx or dy or dc]
    return side, sorted(steps, key=lambda s: -(min(s[0], side - s[0]) + min(s[1], side - s[1])))


def rounded(v):
    return v.astype(bf16).astype(f32)


def split3(v):
    a = rounded(v)
    b = rounded(v - a)
    return a, b, rounded(v - a - b)


def rank_keys(slots):
    lane = lax.broadcasted_iota(jnp.int32, slots.shape, 1)
    group = lax.broadcasted_iota(jnp.int32, slots.shape, 0)
    place = lane & (CAP - 1)
    dup = jnp.zeros(slots.shape, jnp.int32)
    for s in range(1, CAP):
        same = (pltpu.roll(slots, s, 1) == slots) & (place >= s)
        dup = jnp.where(same, 1, dup)
    first = (dup == 0) & (slots >= 0)
    named = jnp.where(first, slots, 1 << 20)
    rank = jnp.zeros(slots.shape, jnp.int32)
    for s in range(1, CAP):
        below = (pltpu.roll(named, s, 1) < slots) & (place >= s)
        rank = rank + jnp.where(below, 1, 0)
        below = (pltpu.roll(named, 128 - s, 1) < slots) & (place < CAP - s)
        rank = rank + jnp.where(below, 1, 0)
    key = jnp.where(slots >= 0, group * (128 // CAP * UNIQ) + (lane >> 4) * UNIQ + rank, -1)
    return key, first


def exchange_kernel(
    n_hx, n_nb, slots_hbm, pos_hbm, frc_hbm, counts_hbm, nbr_hbm, src_hbm, rows_hbm, ops_hbm,
    prod_ref, pick_ref, vel_ref,
    slots_ref, pos_ref, frc_ref, counts_ref, nbr_ref, src_ref,
    rows, ops, send, recv, gathered, raw, alive, yq, feat, xtgt, moments,
    send_sem, recv_sem, halo_send, halo_recv, small_sem, rows_sem, ops_sem,
):
    hx, nb = lax.axis_index("hx"), lax.axis_index("nb")
    after, before = lax.rem(nb + 1, n_nb), lax.rem(nb + n_nb - 1, n_nb)
    coeffs = rows_hbm.shape[0]
    leaves, lanes = pos_ref.shape[1], pos_ref.shape[2]
    half = send.shape[2]
    n_keys = n_hx * UNIQ

    small = [
        pltpu.make_async_copy(a, b, small_sem.at[k])
        for k, (a, b) in enumerate(
            (
                (slots_hbm, slots_ref), (counts_hbm, counts_ref), (pos_hbm, pos_ref), (frc_hbm, frc_ref),
                (nbr_hbm, nbr_ref), (src_hbm, src_ref),
            )
        )
    ]
    for c in small[:4]:
        c.start()
    rows_copy = pltpu.make_async_copy(rows_hbm, rows.at[pl.ds(0, coeffs), :], rows_sem)
    rows_copy.start()
    for c in small[4:]:
        c.start()

    side, steps = peer_steps(n_hx)
    at_x, at_y, at_c = hx // (2 * side), lax.rem(hx // 2, side), lax.rem(hx, 2)

    def peer(dx, dy, dc):
        return lax.rem(at_x + dx, side) * (2 * side) + lax.rem(at_y + dy, side) * 2 + lax.rem(at_c + dc, 2)

    barrier = pltpu.get_barrier_semaphore()
    for step in steps:
        pl.semaphore_signal(barrier, inc=1, device_id={"hx": peer(*step)}, device_id_type=MESH)
    for other in (after, before):
        pl.semaphore_signal(barrier, inc=1, device_id={"nb": other}, device_id_type=MESH)

    ops_copies = [pltpu.make_async_copy(ops_hbm.at[t], ops.at[t], ops_sem.at[t]) for t in range(ops.shape[0])]

    small[0].wait()
    slots = slots_ref[...]
    four = [slots[:, g * lanes : (g + 1) * lanes] for g in range(4)]
    slots8 = jnp.concatenate(four + four, axis=0)
    key, first = rank_keys(slots8)
    key_ids = lax.broadcasted_iota(jnp.int32, (n_keys, lanes), 0)
    choose = jnp.concatenate(
        [jnp.where(key_ids == key[g : g + 1, :], 1.0, 0.0).astype(bf16) for g in range(4)], axis=1
    )
    high = jnp.where(first, slots8 >> 5, 0).astype(f32)
    low = jnp.where(first, slots8 & 31, 0).astype(f32)
    zero6 = jnp.zeros((6, lanes), f32)
    marks = jnp.concatenate(
        [jnp.concatenate([high[g : g + 1], low[g : g + 1], zero6], axis=0) for g in range(4)], axis=1
    )
    rows[coeffs : coeffs + 8, :] = marks.astype(bf16)
    rows[coeffs + 8 :, :] = jnp.zeros((rows.shape[0] - coeffs - 8, rows.shape[1]), bf16)

    for c in small[1:4]:
        c.wait()
    lane_ids = lax.broadcasted_iota(jnp.int32, (1, lanes), 1)
    for l in range(leaves):
        live = jnp.where(lane_ids < counts_ref[0, l], 1.0, 0.0).astype(f32)
        alive[l : l + 1, :] = live
        block = [pos_ref[c, l : l + 1, :] for c in range(3)]
        block += [frc_ref[c, l : l + 1, :] * live for c in range(3)]
        block += [jnp.ones((1, lanes), f32), jnp.zeros((1, lanes), f32)]
        raw[1, l] = jnp.concatenate(block, axis=0)

    rows_copy.wait()
    for c in ops_copies:
        c.start()
    sums = lax.dot_general(choose, rows[...], NT_DIMS, preferred_element_type=f32)
    upper = lax.broadcasted_iota(jnp.int32, (8, half), 0) < UNIQ
    for v in range(n_hx // 2):
        left, right = sums[8 * v : 8 * v + 8, :half], sums[8 * v : 8 * v + 8, half:]
        send[2 * v] = jnp.where(upper, left, pltpu.roll(right, UNIQ, 0)).astype(bf16)
        send[2 * v + 1] = jnp.where(upper, pltpu.roll(left, UNIQ, 0), right).astype(bf16)

    pl.semaphore_wait(barrier, n_hx - 1 + 2)

    def halo(k, target):
        return pltpu.make_async_remote_copy(
            src_ref=raw.at[1], dst_ref=raw.at[k], send_sem=halo_send.at[k // 2], recv_sem=halo_recv.at[k // 2],
            device_id={"nb": target}, device_id_type=MESH,
        )

    up, down = halo(0, after), halo(2, before)
    up.start()
    down.start()

    def chunk(d, step):
        target = peer(*step)
        return pltpu.make_async_remote_copy(
            src_ref=send.at[target], dst_ref=recv.at[hx], send_sem=send_sem.at[d], recv_sem=recv_sem.at[d],
            device_id={"hx": target}, device_id_type=MESH,
        )

    chunks = [chunk(d, step) for d, step in enumerate(steps)]
    for c in chunks:
        c.start()
    recv[hx] = send[hx]

    row8 = lax.broadcasted_iota(jnp.int32, (leaves, 8, lanes), 1)
    zero8 = jnp.zeros((leaves, 8, lanes), f32)
    is_pos, is_frc = row8 < 3, (row8 >= 3) & (row8 < 6)

    def pos_sum(v):
        return jnp.sum(jnp.where(is_pos, v, 0.0), axis=1, keepdims=True)

    own = raw[1]
    own_high = rounded(own)
    own_low = rounded(own - own_high)
    x_sum = own_high + own_low
    t1, t2, t3 = split3(pos_sum(x_sum * x_sum) + EPS)
    two_high, two_low = -2.0 * own_high, -2.0 * own_low
    x_table = jnp.concatenate(
        [
            jnp.where(is_pos, two_high, jnp.where(is_frc, pltpu.roll(two_high, 3, 1), jnp.where(row8 == 6, t1, t2))),
            jnp.where(is_pos, two_low, jnp.where(is_frc, pltpu.roll(two_low, 3, 1), jnp.where(row8 == 6, t3, 0.0))),
            jnp.where(is_pos, 1.0, zero8),
            zero8,
        ],
        axis=1,
    )
    xtgt[...] = jnp.swapaxes(x_table, 1, 2).astype(bf16)

    def source_side(k, mask):
        src = raw[k]
        if mask is not None:
            src = jnp.where(is_frc, src * mask, src)
        at = pl.ds(k * leaves, leaves)
        s_high = rounded(src)
        s_low = rounded(src - s_high)
        s_sum = s_high + s_low
        y1, y2, y3 = split3(pos_sum(s_sum * s_sum))
        pairs = jnp.where(is_pos, s_high, jnp.where(is_frc, pltpu.roll(s_low, 3, 1), 1.0))
        squares = jnp.where(row8 == 0, y1, jnp.where(row8 == 1, y2, jnp.where(row8 == 2, y3, 0.0)))
        yq[at] = jnp.concatenate([pairs, pairs, squares, zero8], axis=1).astype(bf16)
        square = pos_sum(src * src)
        f_at0, f_at6 = pltpu.roll(src, 5, 1), pltpu.roll(src, 3, 1)
        f_dot_y = pos_sum(src * f_at0)
        z = src[:, 2:3, :]
        products = jnp.where(is_pos, f_at0, jnp.where(is_frc, src, f_at6)) * jnp.where(
            is_pos, src[:, 0:1, :], jnp.where(is_frc, src[:, 1:2, :], z)
        )
        second = pltpu.roll(src, 1, 1) * square + pltpu.roll(src, 4, 1) * f_dot_y
        others = jnp.where(
            row8 == 0, f_at6 * z, jnp.where(row8 < 4, pltpu.roll(src, 6, 1), jnp.where(row8 < 7, second, 0.0))
        )
        a, b = split3(products), split3(others)
        feat[at] = jnp.concatenate([a[0], b[0], a[1], b[1], a[2], b[2]], axis=1).astype(bf16)

    source_side(1, None)
    up.wait_recv()
    source_side(0, jnp.where(nb > 0, 1.0, 0.0).astype(f32))
    down.wait_recv()
    source_side(2, jnp.where(nb < n_nb - 1, 1.0, 0.0).astype(f32))
    small[4].wait()

    def leaf(i, c):
        which = [nbr_ref[n, i] for n in range(nbr_ref.shape[0])]
        q = jnp.dot(xtgt[i], jnp.concatenate([yq[n] for n in which], axis=1), preferred_element_type=f32)
        r = lax.rsqrt(q)
        w = (r * r * r).astype(bf16)
        m = lax.dot_general(
            jnp.concatenate([feat[n] for n in which], axis=1), w, NT_DIMS, preferred_element_type=f32
        )
        moments[i] = m[:16] + m[16:32] + m[32:]
        return c

    lax.fori_loop(0, leaves, leaf, 0, unroll=True)
    m = [moments[:, k, :] for k in range(15)]
    x = [pos_ref[c] for c in range(3)]
    two_e = x[0] * x[0] + x[1] * x[1] + x[2] * x[2] + 2.0 * EPS
    along = x[0] * m[9] + x[1] * m[10] + x[2] * m[11] - (m[0] + m[4] + m[8])
    live = alive[...] * SCALE
    for c in range(3):
        u = two_e * m[9 + c] + x[c] * along + m[12 + c]
        for b in range(3):
            u = u - x[b] * (2.0 * m[3 * b + c] + m[3 * c + b])
        vel_ref[c] = u * live

    for c in chunks:
        c.wait_recv()
    for v in range(n_hx // 4):
        lefts, rights = [], []
        for k in (4 * v, 4 * v + 2):
            a, b = recv[k].astype(f32), recv[k + 1].astype(f32)
            lefts.append(jnp.where(upper, a, pltpu.roll(b, UNIQ, 0)))
            rights.append(jnp.where(upper, pltpu.roll(a, UNIQ, 0), b))
        gathered[16 * v : 16 * (v + 1), :half] = jnp.concatenate(lefts, axis=0).astype(bf16)
        gathered[16 * v : 16 * (v + 1), half:] = jnp.concatenate(rights, axis=0).astype(bf16)
    whose = gathered[:, coeffs : coeffs + 2].astype(f32)
    ids = (whose[:, 0:1] * 32.0 + whose[:, 1:2]).astype(jnp.int32)
    small[5].wait()
    for c in ops_copies:
        c.wait()
    for t in range(ops.shape[0]):
        part = jnp.dot(gathered[:, :coeffs], ops[t], preferred_element_type=f32)
        prod_ref[:, t * n_keys : (t + 1) * n_keys] = part.T.astype(bf16)
        pick_ref[t * n_keys : (t + 1) * n_keys, :] = jnp.where(ids == src_ref[t : t + 1, :], 1.0, 0.0).astype(bf16)

    for c in chunks:
        c.wait_send()
    up.wait_send()
    down.wait_send()


def select_kernel(parts, prod_ref, pick_ref, vel_in, out_hbm, vel_out, buffer, sems):
    vel_out[...] = vel_in[...]
    copies, at = [], 0
    for k, size in enumerate(parts):
        rows = slice(at, at + size)
        buffer[rows, :] = jnp.dot(prod_ref[rows, :], pick_ref[...], preferred_element_type=f32).astype(bf16)
        copies.append(pltpu.make_async_copy(buffer.at[pl.ds(at, size)], out_hbm.at[pl.ds(at, size)], sems.at[k]))
        copies[-1].start()
        at += size
    for c in copies:
        c.wait()


def on_device(
    n_hx, n_nb, partial_multipoles, shared_slots, m2l_sources, m2l_ops, positions, forces, leaf_counts, neighbours
):
    rows_t = partial_multipoles[0].T
    coeffs, n_rows = rows_t.shape
    n_dirs, owned = m2l_sources.shape[1:]
    n_near = neighbours.shape[1]
    leaves = leaf_counts.shape[1]
    lanes = positions.shape[2] // leaves
    n_keys = n_hx * UNIQ
    vmem = pl.BlockSpec(memory_space=pltpu.VMEM)
    hbm = pl.BlockSpec(memory_space=pltpu.HBM)
    half = pl.cdiv(coeffs + 8, 256) * 128
    i32 = jnp.int32
    prod, pick, vel = pl.pallas_call(
        functools.partial(exchange_kernel, n_hx, n_nb),
        out_shape=(
            jax.ShapeDtypeStruct((coeffs, n_dirs * n_keys), bf16),
            jax.ShapeDtypeStruct((n_dirs * n_keys, owned), bf16),
            jax.ShapeDtypeStruct((3, leaves, lanes), f32),
        ),
        in_specs=[hbm] * 8,
        out_specs=(vmem, vmem, vmem),
        scratch_shapes=[
            pltpu.VMEM((1, n_rows), i32),
            pltpu.VMEM((3, leaves, lanes), f32),
            pltpu.VMEM((3, leaves, lanes), f32),
            pltpu.SMEM((1, leaves), i32),
            pltpu.SMEM((n_near, leaves), i32),
            pltpu.VMEM((n_dirs, owned), i32),
            pltpu.VMEM((2 * half, n_rows), bf16),
            pltpu.VMEM((n_dirs, coeffs, coeffs), bf16),
            pltpu.VMEM((n_hx, 2 * UNIQ, half), bf16),
            pltpu.VMEM((n_hx, 2 * UNIQ, half), bf16),
            pltpu.VMEM((n_keys, 2 * half), bf16),
            pltpu.VMEM((3, leaves, 8, lanes), f32),
            pltpu.VMEM((leaves, lanes), f32),
            pltpu.VMEM((3 * leaves, QROWS, lanes), bf16),
            pltpu.VMEM((3 * leaves, FROWS, lanes), bf16),
            pltpu.VMEM((leaves, lanes, QROWS), bf16),
            pltpu.VMEM((leaves, 16, lanes), f32),
            pltpu.SemaphoreType.DMA((n_hx,)),
            pltpu.SemaphoreType.DMA((n_hx,)),
            pltpu.SemaphoreType.DMA((2,)),
            pltpu.SemaphoreType.DMA((2,)),
            pltpu.SemaphoreType.DMA((6,)),
            pltpu.SemaphoreType.DMA,
            pltpu.SemaphoreType.DMA((n_dirs,)),
        ],
        compiler_params=pltpu.CompilerParams(
            collective_id=0, has_side_effects=True, vmem_limit_bytes=48 * 1024 * 1024
        ),
        name="exchange",
    )(
        *[
            pltpu.with_memory_space_constraint(v, pltpu.HBM)
            for v in (
                shared_slots, positions.reshape(3, leaves, lanes), forces.reshape(3, leaves, lanes), leaf_counts,
                neighbours[0], m2l_sources[0], rows_t, m2l_ops,
            )
        ]
    )
    step = pl.cdiv(coeffs, 8 * 8) * 8
    parts = [min(step, coeffs - k) for k in range(0, coeffs, step)]
    out_t, velocity = pl.pallas_call(
        functools.partial(select_kernel, parts),
        out_shape=(
            jax.ShapeDtypeStruct((coeffs, owned), bf16),
            jax.ShapeDtypeStruct((3, leaves, lanes), f32),
        ),
        in_specs=[vmem, vmem, vmem],
        out_specs=(pl.BlockSpec(memory_space=pl.ANY), vmem),
        scratch_shapes=[pltpu.VMEM((coeffs, owned), bf16), pltpu.SemaphoreType.DMA((len(parts),))],
        compiler_params=pltpu.CompilerParams(vmem_limit_bytes=16 * 1024 * 1024),
        name="select",
    )(prod, pick, vel)
    return out_t.T[None], velocity.reshape(1, 3, leaves * lanes)


def solution(mesh):
    placed = (
        P("nb", "hx", None),
        P("nb", "hx"),
        P("nb", None, "hx"),
        P(),
        P("nb", None, "hx"),
        P("nb", None, "hx"),
        P("nb", "hx"),
        P("nb", None, "hx"),
    )
    return jax.shard_map(
        functools.partial(on_device, mesh.shape["hx"], mesh.shape["nb"]),
        mesh=mesh,
        in_specs=placed,
        out_specs=(P("nb", "hx", None), P("nb", None, "hx")),
        check_vma=False,
    )
```

```python
import functools
import math

import jax
import jax.numpy as jnp
from jax import lax
from jax.experimental import pallas as pl
from jax.experimental.pallas import tpu as pltpu
from jax.sharding import PartitionSpec as P

EPS = 0.01
SCALE = 1.0 / (8.0 * math.pi)
MESH = pl.DeviceIdType.MESH
UNIQ = 4
CAP = 16
QROWS = 32
FROWS = 48
f32 = jnp.float32
bf16 = jnp.bfloat16
NT_DIMS = (((1,), (1,)), ((), ()))


def peer_steps(n_hx):
    side = math.isqrt(n_hx // 2)
    steps = [(dx, dy, dc) for dx in range(side) for dy in range(side) for dc in range(2) if dx or dy or dc]
    return side, sorted(steps, key=lambda s: -(min(s[0], side - s[0]) + min(s[1], side - s[1])))


def rounded(v):
    return v.astype(bf16).astype(f32)


def split3(v):
    a = rounded(v)
    b = rounded(v - a)
    return a, b, rounded(v - a - b)


def rank_keys(slots):
    lane = lax.broadcasted_iota(jnp.int32, slots.shape, 1)
    group = lax.broadcasted_iota(jnp.int32, slots.shape, 0)
    place = lane & (CAP - 1)
    dup = jnp.zeros(slots.shape, jnp.int32)
    for s in range(1, CAP):
        same = (pltpu.roll(slots, s, 1) == slots) & (place >= s)
        dup = jnp.where(same, 1, dup)
    first = (dup == 0) & (slots >= 0)
    named = jnp.where(first, slots, 1 << 20)
    rank = jnp.zeros(slots.shape, jnp.int32)
    for s in range(1, CAP):
        below = (pltpu.roll(named, s, 1) < slots) & (place >= s)
        rank = rank + jnp.where(below, 1, 0)
        below = (pltpu.roll(named, 128 - s, 1) < slots) & (place < CAP - s)
        rank = rank + jnp.where(below, 1, 0)
    key = jnp.where(slots >= 0, group * (128 // CAP * UNIQ) + (lane >> 4) * UNIQ + rank, -1)
    return key, first


def exchange_kernel(
    n_hx, n_nb, slots_hbm, pos_hbm, frc_hbm, counts_hbm, nbr_hbm, src_hbm, rows_hbm, ops_hbm,
    gathered, ops, src_ref, vel_ref,
    slots_ref, pos_ref, frc_ref, counts_ref, nbr_ref,
    rows, send, recv, raw, alive, yq, feat, xtgt, moments,
    send_sem, recv_sem, halo_send, halo_recv, small_sem, rows_sem, ops_sem,
):
    hx, nb = lax.axis_index("hx"), lax.axis_index("nb")
    after, before = lax.rem(nb + 1, n_nb), lax.rem(nb + n_nb - 1, n_nb)
    coeffs = rows_hbm.shape[0]
    leaves, lanes = pos_ref.shape[1], pos_ref.shape[2]
    half = send.shape[2]
    n_keys = n_hx * UNIQ

    small = [
        pltpu.make_async_copy(a, b, small_sem.at[k])
        for k, (a, b) in enumerate(
            (
                (slots_hbm, slots_ref), (counts_hbm, counts_ref), (pos_hbm, pos_ref), (frc_hbm, frc_ref),
                (nbr_hbm, nbr_ref), (src_hbm, src_ref),
            )
        )
    ]
    for c in small[:4]:
        c.start()
    rows_copy = pltpu.make_async_copy(rows_hbm, rows.at[pl.ds(0, coeffs), :], rows_sem)
    rows_copy.start()
    for c in small[4:]:
        c.start()

    side, steps = peer_steps(n_hx)
    at_x, at_y, at_c = hx // (2 * side), lax.rem(hx // 2, side), lax.rem(hx, 2)

    def peer(dx, dy, dc):
        return lax.rem(at_x + dx, side) * (2 * side) + lax.rem(at_y + dy, side) * 2 + lax.rem(at_c + dc, 2)

    barrier = pltpu.get_barrier_semaphore()
    for step in steps:
        pl.semaphore_signal(barrier, inc=1, device_id={"hx": peer(*step)}, device_id_type=MESH)
    for other in (after, before):
        pl.semaphore_signal(barrier, inc=1, device_id={"nb": other}, device_id_type=MESH)

    ops_copies = [pltpu.make_async_copy(ops_hbm.at[t], ops.at[t], ops_sem.at[t]) for t in range(ops.shape[0])]

    small[0].wait()
    slots = slots_ref[...]
    four = [slots[:, g * lanes : (g + 1) * lanes] for g in range(4)]
    slots8 = jnp.concatenate(four + four, axis=0)
    key, first = rank_keys(slots8)
    key_ids = lax.broadcasted_iota(jnp.int32, (n_keys, lanes), 0)
    choose = jnp.concatenate(
        [jnp.where(key_ids == key[g : g + 1, :], 1.0, 0.0).astype(bf16) for g in range(4)], axis=1
    )
    high = jnp.where(first, slots8 >> 5, 0).astype(f32)
    low = jnp.where(first, slots8 & 31, 0).astype(f32)
    zero6 = jnp.zeros((6, lanes), f32)
    marks = jnp.concatenate(
        [jnp.concatenate([high[g : g + 1], low[g : g + 1], zero6], axis=0) for g in range(4)], axis=1
    )
    rows[coeffs : coeffs + 8, :] = marks.astype(bf16)
    rows[coeffs + 8 :, :] = jnp.zeros((rows.shape[0] - coeffs - 8, rows.shape[1]), bf16)

    for c in small[1:4]:
        c.wait()
    lane_ids = lax.broadcasted_iota(jnp.int32, (1, lanes), 1)
    for l in range(leaves):
        live = jnp.where(lane_ids < counts_ref[0, l], 1.0, 0.0).astype(f32)
        alive[l : l + 1, :] = live
        block = [pos_ref[c, l : l + 1, :] for c in range(3)]
        block += [frc_ref[c, l : l + 1, :] * live for c in range(3)]
        block += [jnp.ones((1, lanes), f32), jnp.zeros((1, lanes), f32)]
        raw[1, l] = jnp.concatenate(block, axis=0)

    rows_copy.wait()
    for c in ops_copies:
        c.start()
    sums = lax.dot_general(choose, rows[...], NT_DIMS, preferred_element_type=f32)
    upper = lax.broadcasted_iota(jnp.int32, (8, half), 0) < UNIQ
    for v in range(n_hx // 2):
        left, right = sums[8 * v : 8 * v + 8, :half], sums[8 * v : 8 * v + 8, half:]
        send[2 * v] = jnp.where(upper, left, pltpu.roll(right, UNIQ, 0)).astype(bf16)
        send[2 * v + 1] = jnp.where(upper, pltpu.roll(left, UNIQ, 0), right).astype(bf16)

    pl.semaphore_wait(barrier, n_hx - 1 + 2)

    def halo(k, target):
        return pltpu.make_async_remote_copy(
            src_ref=raw.at[1], dst_ref=raw.at[k], send_sem=halo_send.at[k // 2], recv_sem=halo_recv.at[k // 2],
            device_id={"nb": target}, device_id_type=MESH,
        )

    up, down = halo(0, after), halo(2, before)
    up.start()
    down.start()

    def chunk(d, step):
        target = peer(*step)
        return pltpu.make_async_remote_copy(
            src_ref=send.at[target], dst_ref=recv.at[hx], send_sem=send_sem.at[d], recv_sem=recv_sem.at[d],
            device_id={"hx": target}, device_id_type=MESH,
        )

    chunks = [chunk(d, step) for d, step in enumerate(steps)]
    for c in chunks:
        c.start()
    recv[hx] = send[hx]

    row8 = lax.broadcasted_iota(jnp.int32, (leaves, 8, lanes), 1)
    zero8 = jnp.zeros((leaves, 8, lanes), f32)
    is_pos, is_frc = row8 < 3, (row8 >= 3) & (row8 < 6)

    def pos_sum(v):
        return jnp.sum(jnp.where(is_pos, v, 0.0), axis=1, keepdims=True)

    own = raw[1]
    own_high = rounded(own)
    own_low = rounded(own - own_high)
    x_sum = own_high + own_low
    t1, t2, t3 = split3(pos_sum(x_sum * x_sum) + EPS)
    two_high, two_low = -2.0 * own_high, -2.0 * own_low
    x_table = jnp.concatenate(
        [
            jnp.where(is_pos, two_high, jnp.where(is_frc, pltpu.roll(two_high, 3, 1), jnp.where(row8 == 6, t1, t2))),
            jnp.where(is_pos, two_low, jnp.where(is_frc, pltpu.roll(two_low, 3, 1), jnp.where(row8 == 6, t3, 0.0))),
            jnp.where(is_pos, 1.0, zero8),
            zero8,
        ],
        axis=1,
    )
    xtgt[...] = jnp.swapaxes(x_table, 1, 2).astype(bf16)

    def source_side(k, mask):
        src = raw[k]
        if mask is not None:
            src = jnp.where(is_frc, src * mask, src)
        at = pl.ds(k * leaves, leaves)
        s_high = rounded(src)
        s_low = rounded(src - s_high)
        s_sum = s_high + s_low
        y1, y2, y3 = split3(pos_sum(s_sum * s_sum))
        pairs = jnp.where(is_pos, s_high, jnp.where(is_frc, pltpu.roll(s_low, 3, 1), 1.0))
        squares = jnp.where(row8 == 0, y1, jnp.where(row8 == 1, y2, jnp.where(row8 == 2, y3, 0.0)))
        yq[at] = jnp.concatenate([pairs, pairs, squares, zero8], axis=1).astype(bf16)
        square = pos_sum(src * src)
        f_at0, f_at6 = pltpu.roll(src, 5, 1), pltpu.roll(src, 3, 1)
        f_dot_y = pos_sum(src * f_at0)
        z = src[:, 2:3, :]
        products = jnp.where(is_pos, f_at0, jnp.where(is_frc, src, f_at6)) * jnp.where(
            is_pos, src[:, 0:1, :], jnp.where(is_frc, src[:, 1:2, :], z)
        )
        second = pltpu.roll(src, 1, 1) * square + pltpu.roll(src, 4, 1) * f_dot_y
        others = jnp.where(
            row8 == 0, f_at6 * z, jnp.where(row8 < 4, pltpu.roll(src, 6, 1), jnp.where(row8 < 7, second, 0.0))
        )
        a, b = split3(products), split3(others)
        feat[at] = jnp.concatenate([a[0], b[0], a[1], b[1], a[2], b[2]], axis=1).astype(bf16)

    source_side(1, None)
    up.wait_recv()
    source_side(0, jnp.where(nb > 0, 1.0, 0.0).astype(f32))
    down.wait_recv()
    source_side(2, jnp.where(nb < n_nb - 1, 1.0, 0.0).astype(f32))
    small[4].wait()

    def leaf(i, c):
        which = [nbr_ref[n, i] for n in range(nbr_ref.shape[0])]
        q = jnp.dot(xtgt[i], jnp.concatenate([yq[n] for n in which], axis=1), preferred_element_type=f32)
        r = lax.rsqrt(q)
        w = (r * r * r).astype(bf16)
        m = lax.dot_general(
            jnp.concatenate([feat[n] for n in which], axis=1), w, NT_DIMS, preferred_element_type=f32
        )
        moments[i] = m[:16] + m[16:32] + m[32:]
        return c

    lax.fori_loop(0, leaves, leaf, 0, unroll=True)
    m = [moments[:, k, :] for k in range(15)]
    x = [pos_ref[c] for c in range(3)]
    two_e = x[0] * x[0] + x[1] * x[1] + x[2] * x[2] + 2.0 * EPS
    along = x[0] * m[9] + x[1] * m[10] + x[2] * m[11] - (m[0] + m[4] + m[8])
    live = alive[...] * SCALE
    for c in range(3):
        u = two_e * m[9 + c] + x[c] * along + m[12 + c]
        for b in range(3):
            u = u - x[b] * (2.0 * m[3 * b + c] + m[3 * c + b])
        vel_ref[c] = u * live

    for c in chunks:
        c.wait_recv()
    for v in range(n_hx // 4):
        lefts, rights = [], []
        for k in (4 * v, 4 * v + 2):
            a, b = recv[k].astype(f32), recv[k + 1].astype(f32)
            lefts.append(jnp.where(upper, a, pltpu.roll(b, UNIQ, 0)))
            rights.append(jnp.where(upper, pltpu.roll(a, UNIQ, 0), b))
        gathered[16 * v : 16 * (v + 1), :half] = jnp.concatenate(lefts, axis=0).astype(bf16)
        gathered[16 * v : 16 * (v + 1), half:] = jnp.concatenate(rights, axis=0).astype(bf16)
    small[5].wait()
    for c in ops_copies:
        c.wait()
    for c in chunks:
        c.wait_send()
    up.wait_send()
    down.wait_send()


def translate_kernel(parts, rows_ref, ops_ref, src_ref, vel_in, out_hbm, vel_hbm, pick, buffer, sems, vel_sem):
    vel_copy = pltpu.make_async_copy(vel_in, vel_hbm, vel_sem)
    vel_copy.start()
    n_dirs, coeffs = ops_ref.shape[:2]
    n_keys = rows_ref.shape[0]
    whose = rows_ref[:, coeffs : coeffs + 2].astype(f32)
    ids = (whose[:, 0:1] * 32.0 + whose[:, 1:2]).astype(jnp.int32)
    for t in range(n_dirs):
        pick[t * n_keys : (t + 1) * n_keys, :] = jnp.where(ids == src_ref[t : t + 1, :], 1.0, 0.0).astype(bf16)

    def product(at, size):
        held = rows_ref[:, :coeffs]
        both = [jnp.dot(held, ops_ref[t, :, at : at + size], preferred_element_type=f32) for t in range(n_dirs)]
        return jnp.concatenate(both, axis=0).T.astype(bf16)

    starts = [sum(parts[:k]) for k in range(len(parts))]
    copies = []
    ready = product(0, parts[0])
    for k, (at, size) in enumerate(zip(starts, parts)):
        later = product(starts[k + 1], parts[k + 1]) if k + 1 < len(parts) else None
        buffer[at : at + size, :] = jnp.dot(ready, pick[...], preferred_element_type=f32).astype(bf16)
        copies.append(pltpu.make_async_copy(buffer.at[pl.ds(at, size)], out_hbm.at[pl.ds(at, size)], sems.at[k]))
        copies[-1].start()
        ready = later
    for c in copies:
        c.wait()
    vel_copy.wait()


def on_device(
    n_hx, n_nb, partial_multipoles, shared_slots, m2l_sources, m2l_ops, positions, forces, leaf_counts, neighbours
):
    rows_t = partial_multipoles[0].T
    coeffs, n_rows = rows_t.shape
    n_dirs, owned = m2l_sources.shape[1:]
    n_near = neighbours.shape[1]
    leaves = leaf_counts.shape[1]
    lanes = positions.shape[2] // leaves
    n_keys = n_hx * UNIQ
    vmem = pl.BlockSpec(memory_space=pltpu.VMEM)
    hbm = pl.BlockSpec(memory_space=pltpu.HBM)
    half = pl.cdiv(coeffs + 8, 256) * 128
    i32 = jnp.int32
    summed, ops, sources, vel = pl.pallas_call(
        functools.partial(exchange_kernel, n_hx, n_nb),
        out_shape=(
            jax.ShapeDtypeStruct((n_keys, 2 * half), bf16),
            jax.ShapeDtypeStruct((n_dirs, coeffs, coeffs), bf16),
            jax.ShapeDtypeStruct((n_dirs, owned), i32),
            jax.ShapeDtypeStruct((3, leaves, lanes), f32),
        ),
        in_specs=[hbm] * 8,
        out_specs=(vmem, vmem, vmem, vmem),
        scratch_shapes=[
            pltpu.VMEM((1, n_rows), i32),
            pltpu.VMEM((3, leaves, lanes), f32),
            pltpu.VMEM((3, leaves, lanes), f32),
            pltpu.SMEM((1, leaves), i32),
            pltpu.SMEM((n_near, leaves), i32),
            pltpu.VMEM((2 * half, n_rows), bf16),
            pltpu.VMEM((n_hx, 2 * UNIQ, half), bf16),
            pltpu.VMEM((n_hx, 2 * UNIQ, half), bf16),
            pltpu.VMEM((3, leaves, 8, lanes), f32),
            pltpu.VMEM((leaves, lanes), f32),
            pltpu.VMEM((3 * leaves, QROWS, lanes), bf16),
            pltpu.VMEM((3 * leaves, FROWS, lanes), bf16),
            pltpu.VMEM((leaves, lanes, QROWS), bf16),
            pltpu.VMEM((leaves, 16, lanes), f32),
            pltpu.SemaphoreType.DMA((n_hx,)),
            pltpu.SemaphoreType.DMA((n_hx,)),
            pltpu.SemaphoreType.DMA((2,)),
            pltpu.SemaphoreType.DMA((2,)),
            pltpu.SemaphoreType.DMA((6,)),
            pltpu.SemaphoreType.DMA,
            pltpu.SemaphoreType.DMA((n_dirs,)),
        ],
        compiler_params=pltpu.CompilerParams(
            collective_id=0, has_side_effects=True, vmem_limit_bytes=32 * 1024 * 1024
        ),
        name="exchange",
    )(
        *[
            pltpu.with_memory_space_constraint(v, pltpu.HBM)
            for v in (
                shared_slots, positions.reshape(3, leaves, lanes), forces.reshape(3, leaves, lanes), leaf_counts,
                neighbours[0], m2l_sources[0], rows_t, m2l_ops,
            )
        ]
    )
    parts = [min(256, coeffs - k) for k in range(0, coeffs, 256)]
    out_t, velocity = pl.pallas_call(
        functools.partial(translate_kernel, parts),
        out_shape=(
            jax.ShapeDtypeStruct((coeffs, owned), bf16),
            jax.ShapeDtypeStruct((3, leaves, lanes), f32),
        ),
        in_specs=[vmem] * 4,
        out_specs=(pl.BlockSpec(memory_space=pl.ANY),) * 2,
        scratch_shapes=[
            pltpu.VMEM((n_dirs * n_keys, owned), bf16),
            pltpu.VMEM((coeffs, owned), bf16),
            pltpu.SemaphoreType.DMA((len(parts),)),
            pltpu.SemaphoreType.DMA,
        ],
        compiler_params=pltpu.CompilerParams(vmem_limit_bytes=32 * 1024 * 1024),
        name="translate",
    )(summed, ops, sources, vel)
    return out_t.T[None], velocity.reshape(1, 3, leaves * lanes)


def solution(mesh):
    placed = (
        P("nb", "hx", None),
        P("nb", "hx"),
        P("nb", None, "hx"),
        P(),
        P("nb", None, "hx"),
        P("nb", None, "hx"),
        P("nb", "hx"),
        P("nb", None, "hx"),
    )
    return jax.shard_map(
        functools.partial(on_device, mesh.shape["hx"], mesh.shape["nb"]),
        mesh=mesh,
        in_specs=placed,
        out_specs=(P("nb", "hx", None), P("nb", None, "hx")),
        check_vma=False,
    )
```

```python
import functools
import math

import jax
import jax.numpy as jnp
from jax import lax
from jax.experimental import pallas as pl
from jax.experimental.pallas import tpu as pltpu
from jax.sharding import PartitionSpec as P

EPS = 0.01
SCALE = 1.0 / (8.0 * math.pi)
MESH = pl.DeviceIdType.MESH
UNIQ = 4
CAP = 16
QROWS = 32
FROWS = 48
f32 = jnp.float32
bf16 = jnp.bfloat16
NT_DIMS = (((1,), (1,)), ((), ()))


def peer_steps(n_hx):
    side = math.isqrt(n_hx // 2)
    steps = [(dx, dy, dc) for dx in range(side) for dy in range(side) for dc in range(2) if dx or dy or dc]
    return side, sorted(steps, key=lambda s: -(min(s[0], side - s[0]) + min(s[1], side - s[1])))


def rounded(v):
    return v.astype(bf16).astype(f32)


def split3(v):
    a = rounded(v)
    b = rounded(v - a)
    return a, b, rounded(v - a - b)


def rank_keys(slots):
    lane = lax.broadcasted_iota(jnp.int32, slots.shape, 1)
    group = lax.broadcasted_iota(jnp.int32, slots.shape, 0)
    place = lane & (CAP - 1)
    dup = jnp.zeros(slots.shape, jnp.int32)
    for s in range(1, CAP):
        same = (pltpu.roll(slots, s, 1) == slots) & (place >= s)
        dup = jnp.where(same, 1, dup)
    first = (dup == 0) & (slots >= 0)
    named = jnp.where(first, slots, 1 << 20)
    rank = jnp.zeros(slots.shape, jnp.int32)
    for s in range(1, CAP):
        below = (pltpu.roll(named, s, 1) < slots) & (place >= s)
        rank = rank + jnp.where(below, 1, 0)
        below = (pltpu.roll(named, 128 - s, 1) < slots) & (place < CAP - s)
        rank = rank + jnp.where(below, 1, 0)
    key = jnp.where(slots >= 0, group * (128 // CAP * UNIQ) + (lane >> 4) * UNIQ + rank, -1)
    return key, first


def exchange_kernel(
    n_hx, n_nb, slots_hbm, pos_hbm, frc_hbm, counts_hbm, nbr_hbm, src_hbm, rows_hbm, ops_hbm,
    gathered, ops, src_ref, vel_ref,
    slots_ref, pos_ref, frc_ref, counts_ref, nbr_ref,
    rows, send, recv, raw, alive, yq, feat, xtgt, moments,
    send_sem, recv_sem, halo_send, halo_recv, ready_sem, news_sem, all_sem, small_sem, rows_sem, ops_sem,
):
    hx, nb = lax.axis_index("hx"), lax.axis_index("nb")
    after, before = lax.min(nb + 1, n_nb - 1), lax.max(nb - 1, 0)
    has_after, has_before = nb < n_nb - 1, nb > 0
    coeffs = rows_hbm.shape[0]
    leaves, lanes = pos_ref.shape[1], pos_ref.shape[2]
    half = send.shape[2]
    n_keys = n_hx * UNIQ

    small = [
        pltpu.make_async_copy(a, b, small_sem.at[k])
        for k, (a, b) in enumerate(
            (
                (slots_hbm, slots_ref), (counts_hbm, counts_ref), (pos_hbm, pos_ref), (frc_hbm, frc_ref),
                (nbr_hbm, nbr_ref), (src_hbm, src_ref),
            )
        )
    ]
    for c in small[:4]:
        c.start()
    rows_copy = pltpu.make_async_copy(rows_hbm, rows.at[pl.ds(0, coeffs), :], rows_sem)
    rows_copy.start()
    for c in small[4:]:
        c.start()

    side, steps = peer_steps(n_hx)
    at_x, at_y, at_c = hx // (2 * side), lax.rem(hx // 2, side), lax.rem(hx, 2)

    def peer(dx, dy, dc):
        return lax.rem(at_x + dx, side) * (2 * side) + lax.rem(at_y + dy, side) * 2 + lax.rem(at_c + dc, 2)

    barrier = pltpu.get_barrier_semaphore()
    partner = peer(0, 0, 1)
    second = at_c == 1

    for dx, dy in sorted({(dx, dy) for dx, dy, _ in steps} - {(0, 0)}, key=lambda c: -sum(min(d, side - d) for d in c)):
        pl.semaphore_signal(barrier, inc=1, device_id={"hx": peer(dx, dy, 1 - at_c)}, device_id_type=MESH)
    pl.semaphore_signal(barrier, inc=1, device_id={"hx": partner}, device_id_type=MESH)

    @pl.when(has_after)
    def _():
        pl.semaphore_signal(barrier, inc=1, device_id={"hx": hx - at_c, "nb": after}, device_id_type=MESH)

    ops_copies = [pltpu.make_async_copy(ops_hbm.at[t], ops.at[t], ops_sem.at[t]) for t in range(ops.shape[0])]

    for c in small[1:4]:
        c.wait()
    lane_ids = lax.broadcasted_iota(jnp.int32, (1, lanes), 1)
    for l in range(leaves):
        live = jnp.where(lane_ids < counts_ref[0, l], 1.0, 0.0).astype(f32)
        alive[l : l + 1, :] = live
        block = [pos_ref[c, l : l + 1, :] for c in range(3)]
        block += [frc_ref[c, l : l + 1, :] * live for c in range(3)]
        block += [jnp.ones((1, lanes), f32), jnp.zeros((1, lanes), f32)]
        raw[1, l] = jnp.concatenate(block, axis=0)

    edge = jnp.zeros((leaves, 8, lanes), f32)

    @pl.when(nb == 0)
    def _():
        raw[0] = edge

    @pl.when(nb == n_nb - 1)
    def _():
        raw[2] = edge

    def halo(k, target):
        return pltpu.make_async_remote_copy(
            src_ref=raw.at[1], dst_ref=raw.at[k], send_sem=halo_send.at[k // 2], recv_sem=halo_recv.at[k // 2],
            device_id={"nb": target}, device_id_type=MESH,
        )

    up, down = halo(0, after), halo(2, before)

    @pl.when(jnp.logical_not(second))
    def _():
        pl.semaphore_wait(barrier, 1 + 2 * lax.min(nb, 1))

        @pl.when(has_before)
        def _():
            pl.semaphore_signal(news_sem, inc=1, device_id={"hx": partner}, device_id_type=MESH)

    @pl.when(has_before)
    def _():
        @pl.when(second)
        def _():
            pl.semaphore_wait(news_sem, 1)

        down.start()
        pl.semaphore_signal(ready_sem, inc=1, device_id={"nb": before}, device_id_type=MESH)

    small[0].wait()
    slots = slots_ref[...]
    four = [slots[:, g * lanes : (g + 1) * lanes] for g in range(4)]
    slots8 = jnp.concatenate(four + four, axis=0)
    key, first = rank_keys(slots8)
    key_ids = lax.broadcasted_iota(jnp.int32, (n_keys, lanes), 0)
    choose = jnp.concatenate(
        [jnp.where(key_ids == key[g : g + 1, :], 1.0, 0.0).astype(bf16) for g in range(4)], axis=1
    )
    high = jnp.where(first, slots8 >> 5, 0).astype(f32)
    low = jnp.where(first, slots8 & 31, 0).astype(f32)
    zero6 = jnp.zeros((6, lanes), f32)
    marks = jnp.concatenate(
        [jnp.concatenate([high[g : g + 1], low[g : g + 1], zero6], axis=0) for g in range(4)], axis=1
    )
    rows[coeffs : coeffs + 8, :] = marks.astype(bf16)
    rows[coeffs + 8 :, :] = jnp.zeros((rows.shape[0] - coeffs - 8, rows.shape[1]), bf16)

    rows_copy.wait()
    for c in ops_copies:
        c.start()
    sums = lax.dot_general(choose, rows[...], NT_DIMS, preferred_element_type=f32)
    upper = lax.broadcasted_iota(jnp.int32, (8, half), 0) < UNIQ
    for v in range(n_hx // 2):
        left, right = sums[8 * v : 8 * v + 8, :half], sums[8 * v : 8 * v + 8, half:]
        send[2 * v] = jnp.where(upper, left, pltpu.roll(right, UNIQ, 0)).astype(bf16)
        send[2 * v + 1] = jnp.where(upper, pltpu.roll(left, UNIQ, 0), right).astype(bf16)

    @pl.when(second)
    def _():
        pl.semaphore_wait(barrier, n_hx - 1)
        pl.semaphore_signal(all_sem, inc=1, device_id={"hx": partner}, device_id_type=MESH)

    @pl.when(jnp.logical_not(second))
    def _():
        pl.semaphore_wait(all_sem, 1)

    def chunk(step):
        place = (step[0] * side + step[1]) * 2 + step[2]
        target = peer(*step)
        return pltpu.make_async_remote_copy(
            src_ref=send.at[target], dst_ref=recv.at[place], send_sem=send_sem, recv_sem=recv_sem.at[place // 2],
            device_id={"hx": target}, device_id_type=MESH,
        )

    for step in steps:
        chunk(step).start()
    recv[0] = send[hx]

    row8 = lax.broadcasted_iota(jnp.int32, (leaves, 8, lanes), 1)
    zero8 = jnp.zeros((leaves, 8, lanes), f32)
    is_pos, is_frc = row8 < 3, (row8 >= 3) & (row8 < 6)

    def pos_sum(v):
        return jnp.sum(jnp.where(is_pos, v, 0.0), axis=1, keepdims=True)

    own = raw[1]
    own_high = rounded(own)
    own_low = rounded(own - own_high)
    x_sum = own_high + own_low
    t1, t2, t3 = split3(pos_sum(x_sum * x_sum) + EPS)
    two_high, two_low = -2.0 * own_high, -2.0 * own_low
    x_table = jnp.concatenate(
        [
            jnp.where(is_pos, two_high, jnp.where(is_frc, pltpu.roll(two_high, 3, 1), jnp.where(row8 == 6, t1, t2))),
            jnp.where(is_pos, two_low, jnp.where(is_frc, pltpu.roll(two_low, 3, 1), jnp.where(row8 == 6, t3, 0.0))),
            jnp.where(is_pos, 1.0, zero8),
            zero8,
        ],
        axis=1,
    )
    xtgt[...] = jnp.swapaxes(x_table, 1, 2).astype(bf16)

    def source_side(k):
        src = raw[k]
        at = pl.ds(k * leaves, leaves)
        s_high = rounded(src)
        s_low = rounded(src - s_high)
        s_sum = s_high + s_low
        y1, y2, y3 = split3(pos_sum(s_sum * s_sum))
        pairs = jnp.where(is_pos, s_high, jnp.where(is_frc, pltpu.roll(s_low, 3, 1), 1.0))
        squares = jnp.where(row8 == 0, y1, jnp.where(row8 == 1, y2, jnp.where(row8 == 2, y3, 0.0)))
        yq[at] = jnp.concatenate([pairs, pairs, squares, zero8], axis=1).astype(bf16)
        square = pos_sum(src * src)
        f_at0, f_at6 = pltpu.roll(src, 5, 1), pltpu.roll(src, 3, 1)
        f_dot_y = pos_sum(src * f_at0)
        z = src[:, 2:3, :]
        products = jnp.where(is_pos, f_at0, jnp.where(is_frc, src, f_at6)) * jnp.where(
            is_pos, src[:, 0:1, :], jnp.where(is_frc, src[:, 1:2, :], z)
        )
        second = pltpu.roll(src, 1, 1) * square + pltpu.roll(src, 4, 1) * f_dot_y
        others = jnp.where(
            row8 == 0, f_at6 * z, jnp.where(row8 < 4, pltpu.roll(src, 6, 1), jnp.where(row8 < 7, second, 0.0))
        )
        a, b = split3(products), split3(others)
        feat[at] = jnp.concatenate([a[0], b[0], a[1], b[1], a[2], b[2]], axis=1).astype(bf16)

    source_side(1)

    @pl.when(has_after)
    def _():
        pl.semaphore_wait(ready_sem, 1)
        up.start()

    @pl.when(has_before)
    def _():
        up.wait_recv()

    source_side(0)

    @pl.when(has_after)
    def _():
        down.wait_recv()

    source_side(2)
    small[4].wait()

    def leaf(i, c):
        which = [nbr_ref[n, i] for n in range(nbr_ref.shape[0])]
        q = jnp.dot(xtgt[i], jnp.concatenate([yq[n] for n in which], axis=1), preferred_element_type=f32)
        r = lax.rsqrt(q)
        w = (r * r * r).astype(bf16)
        m = lax.dot_general(
            jnp.concatenate([feat[n] for n in which], axis=1), w, NT_DIMS, preferred_element_type=f32
        )
        moments[i] = m[:16] + m[16:32] + m[32:]
        return c

    lax.fori_loop(0, leaves, leaf, 0, unroll=True)
    m = [moments[:, k, :] for k in range(15)]
    x = [pos_ref[c] for c in range(3)]
    two_e = x[0] * x[0] + x[1] * x[1] + x[2] * x[2] + 2.0 * EPS
    along = x[0] * m[9] + x[1] * m[10] + x[2] * m[11] - (m[0] + m[4] + m[8])
    live = alive[...] * SCALE
    for c in range(3):
        u = two_e * m[9 + c] + x[c] * along + m[12 + c]
        for b in range(3):
            u = u - x[b] * (2.0 * m[3 * b + c] + m[3 * c + b])
        vel_ref[c] = u * live

    def arrivals(first, count, sem):
        part = pl.ds(first, count)
        return pltpu.make_async_remote_copy(
            src_ref=send.at[part], dst_ref=recv.at[part], send_sem=send_sem, recv_sem=sem,
            device_id={"hx": peer(0, 0, 1)}, device_id_type=MESH,
        )

    chips = sorted({(dx, dy) for dx, dy, _ in steps}, key=lambda c: sum(min(d, side - d) for d in c))
    for dx, dy in chips:
        k = dx * side + dy
        own_chip = 1 if k == 0 else 0
        arrivals(2 * k + own_chip, 2 - own_chip, recv_sem.at[k]).wait_recv()
        a, b = recv[2 * k].astype(f32), recv[2 * k + 1].astype(f32)
        gathered[8 * k : 8 * k + 8, :half] = jnp.where(upper, a, pltpu.roll(b, UNIQ, 0)).astype(bf16)
        gathered[8 * k : 8 * k + 8, half:] = jnp.where(upper, pltpu.roll(a, UNIQ, 0), b).astype(bf16)
    small[5].wait()
    for c in ops_copies:
        c.wait()
    arrivals(0, n_hx - 1, recv_sem.at[0]).wait_send()

    @pl.when(has_after)
    def _():
        up.wait_send()

    @pl.when(has_before)
    def _():
        down.wait_send()


def translate_kernel(parts, rows_ref, ops_ref, src_ref, vel_in, out_hbm, vel_hbm, pick, buffer, sems, vel_sem):
    vel_copy = pltpu.make_async_copy(vel_in, vel_hbm, vel_sem)
    vel_copy.start()
    n_dirs, coeffs = ops_ref.shape[:2]
    n_keys = rows_ref.shape[0]
    whose = rows_ref[:, coeffs : coeffs + 2].astype(f32)
    ids = (whose[:, 0:1] * 32.0 + whose[:, 1:2]).astype(jnp.int32)
    for t in range(n_dirs):
        pick[t * n_keys : (t + 1) * n_keys, :] = jnp.where(ids == src_ref[t : t + 1, :], 1.0, 0.0).astype(bf16)

    def product(at, size):
        held = rows_ref[:, :coeffs]
        both = [jnp.dot(held, ops_ref[t, :, at : at + size], preferred_element_type=f32) for t in range(n_dirs)]
        return jnp.concatenate(both, axis=0).T.astype(bf16)

    starts = [sum(parts[:k]) for k in range(len(parts))]
    copies = []
    ready = product(0, parts[0])
    for k, (at, size) in enumerate(zip(starts, parts)):
        later = product(starts[k + 1], parts[k + 1]) if k + 1 < len(parts) else None
        buffer[at : at + size, :] = jnp.dot(ready, pick[...], preferred_element_type=f32).astype(bf16)
        copies.append(pltpu.make_async_copy(buffer.at[pl.ds(at, size)], out_hbm.at[pl.ds(at, size)], sems.at[k]))
        copies[-1].start()
        ready = later
    for c in copies:
        c.wait()
    vel_copy.wait()


def on_device(
    n_hx, n_nb, partial_multipoles, shared_slots, m2l_sources, m2l_ops, positions, forces, leaf_counts, neighbours
):
    rows_t = partial_multipoles[0].T
    coeffs, n_rows = rows_t.shape
    n_dirs, owned = m2l_sources.shape[1:]
    n_near = neighbours.shape[1]
    leaves = leaf_counts.shape[1]
    lanes = positions.shape[2] // leaves
    n_keys = n_hx * UNIQ
    vmem = pl.BlockSpec(memory_space=pltpu.VMEM)
    hbm = pl.BlockSpec(memory_space=pltpu.HBM)
    half = pl.cdiv(coeffs + 8, 256) * 128
    i32 = jnp.int32
    summed, ops, sources, vel = pl.pallas_call(
        functools.partial(exchange_kernel, n_hx, n_nb),
        out_shape=(
            jax.ShapeDtypeStruct((n_keys, 2 * half), bf16),
            jax.ShapeDtypeStruct((n_dirs, coeffs, coeffs), bf16),
            jax.ShapeDtypeStruct((n_dirs, owned), i32),
            jax.ShapeDtypeStruct((3, leaves, lanes), f32),
        ),
        in_specs=[hbm] * 8,
        out_specs=(vmem, vmem, vmem, vmem),
        scratch_shapes=[
            pltpu.VMEM((1, n_rows), i32),
            pltpu.VMEM((3, leaves, lanes), f32),
            pltpu.VMEM((3, leaves, lanes), f32),
            pltpu.SMEM((1, leaves), i32),
            pltpu.SMEM((n_near, leaves), i32),
            pltpu.VMEM((2 * half, n_rows), bf16),
            pltpu.VMEM((n_hx, 2 * UNIQ, half), bf16),
            pltpu.VMEM((n_hx, 2 * UNIQ, half), bf16),
            pltpu.VMEM((3, leaves, 8, lanes), f32),
            pltpu.VMEM((leaves, lanes), f32),
            pltpu.VMEM((3 * leaves, QROWS, lanes), bf16),
            pltpu.VMEM((3 * leaves, FROWS, lanes), bf16),
            pltpu.VMEM((leaves, lanes, QROWS), bf16),
            pltpu.VMEM((leaves, 16, lanes), f32),
            pltpu.SemaphoreType.DMA,
            pltpu.SemaphoreType.DMA((n_hx // 2,)),
            pltpu.SemaphoreType.DMA((2,)),
            pltpu.SemaphoreType.DMA((2,)),
            pltpu.SemaphoreType.REGULAR,
            pltpu.SemaphoreType.REGULAR,
            pltpu.SemaphoreType.REGULAR,
            pltpu.SemaphoreType.DMA((6,)),
            pltpu.SemaphoreType.DMA,
            pltpu.SemaphoreType.DMA((n_dirs,)),
        ],
        compiler_params=pltpu.CompilerParams(
            collective_id=0, has_side_effects=True, vmem_limit_bytes=32 * 1024 * 1024
        ),
        name="exchange",
    )(
        *[
            pltpu.with_memory_space_constraint(v, pltpu.HBM)
            for v in (
                shared_slots, positions.reshape(3, leaves, lanes), forces.reshape(3, leaves, lanes), leaf_counts,
                neighbours[0], m2l_sources[0], rows_t, m2l_ops,
            )
        ]
    )
    parts = [min(256, coeffs - k) for k in range(0, coeffs, 256)]
    out_t, velocity = pl.pallas_call(
        functools.partial(translate_kernel, parts),
        out_shape=(
            jax.ShapeDtypeStruct((coeffs, owned), bf16),
            jax.ShapeDtypeStruct((3, leaves, lanes), f32),
        ),
        in_specs=[vmem] * 4,
        out_specs=(pl.BlockSpec(memory_space=pl.ANY),) * 2,
        scratch_shapes=[
            pltpu.VMEM((n_dirs * n_keys, owned), bf16),
            pltpu.VMEM((coeffs, owned), bf16),
            pltpu.SemaphoreType.DMA((len(parts),)),
            pltpu.SemaphoreType.DMA,
        ],
        compiler_params=pltpu.CompilerParams(vmem_limit_bytes=32 * 1024 * 1024),
        name="translate",
    )(summed, ops, sources, vel)
    return out_t.T[None], velocity.reshape(1, 3, leaves * lanes)


def solution(mesh):
    placed = (
        P("nb", "hx", None),
        P("nb", "hx"),
        P("nb", None, "hx"),
        P(),
        P("nb", None, "hx"),
        P("nb", None, "hx"),
        P("nb", "hx"),
        P("nb", None, "hx"),
    )
    return jax.shard_map(
        functools.partial(on_device, mesh.shape["hx"], mesh.shape["nb"]),
        mesh=mesh,
        in_specs=placed,
        out_specs=(P("nb", "hx", None), P("nb", None, "hx")),
        check_vma=False,
    )
```

```python
import functools
import math

import jax
import jax.numpy as jnp
from jax import lax
from jax.experimental import pallas as pl
from jax.experimental.pallas import tpu as pltpu
from jax.sharding import PartitionSpec as P

EPS = 0.01
SCALE = 1.0 / (8.0 * math.pi)
MESH = pl.DeviceIdType.MESH
UNIQ = 4
CAP = 16
QROWS = 32
FROWS = 48
f32 = jnp.float32
bf16 = jnp.bfloat16
NT_DIMS = (((1,), (1,)), ((), ()))


def peer_steps(n_hx):
    side = math.isqrt(n_hx // 2)
    steps = [(dx, dy, dc) for dx in range(side) for dy in range(side) for dc in range(2) if dx or dy or dc]
    return side, sorted(steps, key=lambda s: -(min(s[0], side - s[0]) + min(s[1], side - s[1])))


def rounded(v):
    return v.astype(bf16).astype(f32)


def split3(v):
    a = rounded(v)
    b = rounded(v - a)
    return a, b, rounded(v - a - b)


def rank_keys(slots):
    lane = lax.broadcasted_iota(jnp.int32, slots.shape, 1)
    group = lax.broadcasted_iota(jnp.int32, slots.shape, 0)
    place = lane & (CAP - 1)
    dup = jnp.zeros(slots.shape, jnp.int32)
    for s in range(1, CAP):
        same = (pltpu.roll(slots, s, 1) == slots) & (place >= s)
        dup = jnp.where(same, 1, dup)
    first = (dup == 0) & (slots >= 0)
    named = jnp.where(first, slots, 1 << 20)
    rank = jnp.zeros(slots.shape, jnp.int32)
    for s in range(1, CAP):
        below = (pltpu.roll(named, s, 1) < slots) & (place >= s)
        rank = rank + jnp.where(below, 1, 0)
        below = (pltpu.roll(named, 128 - s, 1) < slots) & (place < CAP - s)
        rank = rank + jnp.where(below, 1, 0)
    key = jnp.where(slots >= 0, group * (128 // CAP * UNIQ) + (lane >> 4) * UNIQ + rank, -1)
    return key, first


def exchange_kernel(
    n_hx, n_nb, slots_hbm, pos_hbm, frc_hbm, counts_hbm, nbr_hbm, src_hbm, rows_hbm, ops_hbm,
    gathered, ops, src_ref, vel_ref,
    slots_ref, pos_ref, frc_ref, counts_ref, nbr_ref,
    rows, send, recv, raw, alive, yq, feat, xtgt, moments,
    send_sem, recv_sem, halo_send, halo_recv, ready_sem, news_sem, all_sem, small_sem, rows_sem, ops_sem,
):
    hx, nb = lax.axis_index("hx"), lax.axis_index("nb")
    after, before = lax.min(nb + 1, n_nb - 1), lax.max(nb - 1, 0)
    has_after, has_before = nb < n_nb - 1, nb > 0
    coeffs = rows_hbm.shape[0]
    leaves, lanes = pos_ref.shape[1], pos_ref.shape[2]
    half = send.shape[2]
    n_keys = n_hx * UNIQ

    small = [
        pltpu.make_async_copy(a, b, small_sem.at[k])
        for k, (a, b) in enumerate(
            (
                (slots_hbm, slots_ref), (counts_hbm, counts_ref), (pos_hbm, pos_ref), (frc_hbm, frc_ref),
                (nbr_hbm, nbr_ref), (src_hbm, src_ref),
            )
        )
    ]
    for c in small[:4]:
        c.start()
    rows_copy = pltpu.make_async_copy(rows_hbm, rows.at[pl.ds(0, coeffs), :], rows_sem)
    rows_copy.start()
    for c in small[4:]:
        c.start()

    side, steps = peer_steps(n_hx)
    at_x, at_y, at_c = hx // (2 * side), lax.rem(hx // 2, side), lax.rem(hx, 2)

    def peer(dx, dy, dc):
        return lax.rem(at_x + dx, side) * (2 * side) + lax.rem(at_y + dy, side) * 2 + lax.rem(at_c + dc, 2)

    barrier = pltpu.get_barrier_semaphore()
    partner = peer(0, 0, 1)
    second = at_c == 1

    for dx, dy in sorted({(dx, dy) for dx, dy, _ in steps} - {(0, 0)}, key=lambda c: -sum(min(d, side - d) for d in c)):
        pl.semaphore_signal(barrier, inc=1, device_id={"hx": peer(dx, dy, 1 - at_c)}, device_id_type=MESH)
    pl.semaphore_signal(barrier, inc=1, device_id={"hx": partner}, device_id_type=MESH)

    @pl.when(has_after)
    def _():
        pl.semaphore_signal(barrier, inc=1, device_id={"hx": hx - at_c, "nb": after}, device_id_type=MESH)

    ops_copies = [pltpu.make_async_copy(ops_hbm.at[t], ops.at[t], ops_sem.at[t]) for t in range(ops.shape[0])]

    for c in small[1:4]:
        c.wait()
    lane_ids = lax.broadcasted_iota(jnp.int32, (1, lanes), 1)
    for l in range(leaves):
        live = jnp.where(lane_ids < counts_ref[0, l], 1.0, 0.0).astype(f32)
        alive[l : l + 1, :] = live
        block = [pos_ref[c, l : l + 1, :] for c in range(3)]
        block += [frc_ref[c, l : l + 1, :] * live for c in range(3)]
        block += [jnp.ones((1, lanes), f32), jnp.zeros((1, lanes), f32)]
        raw[1, l] = jnp.concatenate(block, axis=0)

    edge = jnp.zeros((leaves, 8, lanes), f32)

    @pl.when(nb == 0)
    def _():
        raw[0] = edge

    @pl.when(nb == n_nb - 1)
    def _():
        raw[2] = edge

    def halo(k, target):
        return pltpu.make_async_remote_copy(
            src_ref=raw.at[1], dst_ref=raw.at[k], send_sem=halo_send.at[k // 2], recv_sem=halo_recv.at[k // 2],
            device_id={"nb": target}, device_id_type=MESH,
        )

    up, down = halo(0, after), halo(2, before)

    @pl.when(jnp.logical_not(second))
    def _():
        pl.semaphore_wait(barrier, 1 + 2 * lax.min(nb, 1))

        @pl.when(has_before)
        def _():
            pl.semaphore_signal(news_sem, inc=1, device_id={"hx": partner}, device_id_type=MESH)

    @pl.when(has_before)
    def _():
        @pl.when(second)
        def _():
            pl.semaphore_wait(news_sem, 1)

        down.start()
        pl.semaphore_signal(ready_sem, inc=1, device_id={"nb": before}, device_id_type=MESH)

    small[0].wait()
    slots = slots_ref[...]
    four = [slots[:, g * lanes : (g + 1) * lanes] for g in range(4)]
    slots8 = jnp.concatenate(four + four, axis=0)
    key, first = rank_keys(slots8)
    key_ids = lax.broadcasted_iota(jnp.int32, (n_keys, lanes), 0)
    choose = jnp.concatenate(
        [jnp.where(key_ids == key[g : g + 1, :], 1.0, 0.0).astype(bf16) for g in range(4)], axis=1
    )
    high = jnp.where(first, slots8 >> 5, 0).astype(f32)
    low = jnp.where(first, slots8 & 31, 0).astype(f32)
    zero6 = jnp.zeros((6, lanes), f32)
    marks = jnp.concatenate(
        [jnp.concatenate([high[g : g + 1], low[g : g + 1], zero6], axis=0) for g in range(4)], axis=1
    )
    rows[coeffs : coeffs + 8, :] = marks.astype(bf16)
    rows[coeffs + 8 :, :] = jnp.zeros((rows.shape[0] - coeffs - 8, rows.shape[1]), bf16)

    rows_copy.wait()
    sums = lax.dot_general(choose, rows[...], NT_DIMS, preferred_element_type=f32)
    upper = lax.broadcasted_iota(jnp.int32, (8, half), 0) < UNIQ
    for v in range(n_hx // 2):
        left, right = sums[8 * v : 8 * v + 8, :half], sums[8 * v : 8 * v + 8, half:]
        send[2 * v] = jnp.where(upper, left, pltpu.roll(right, UNIQ, 0)).astype(bf16)
        send[2 * v + 1] = jnp.where(upper, pltpu.roll(left, UNIQ, 0), right).astype(bf16)

    @pl.when(second)
    def _():
        pl.semaphore_wait(barrier, n_hx - 1)
        pl.semaphore_signal(all_sem, inc=1, device_id={"hx": partner}, device_id_type=MESH)

    @pl.when(jnp.logical_not(second))
    def _():
        pl.semaphore_wait(all_sem, 1)

    def chunk(step):
        place = (step[0] * side + step[1]) * 2 + step[2]
        target = peer(*step)
        return pltpu.make_async_remote_copy(
            src_ref=send.at[target], dst_ref=recv.at[place], send_sem=send_sem, recv_sem=recv_sem.at[place // 2],
            device_id={"hx": target}, device_id_type=MESH,
        )

    for step in steps:
        chunk(step).start()
    recv[0] = send[hx]
    for c in ops_copies:
        c.start()

    row8 = lax.broadcasted_iota(jnp.int32, (leaves, 8, lanes), 1)
    zero8 = jnp.zeros((leaves, 8, lanes), f32)
    is_pos, is_frc = row8 < 3, (row8 >= 3) & (row8 < 6)

    def pos_sum(v):
        return jnp.sum(jnp.where(is_pos, v, 0.0), axis=1, keepdims=True)

    own = raw[1]
    own_high = rounded(own)
    own_low = rounded(own - own_high)
    x_sum = own_high + own_low
    t1, t2, t3 = split3(pos_sum(x_sum * x_sum) + EPS)
    two_high, two_low = -2.0 * own_high, -2.0 * own_low
    x_table = jnp.concatenate(
        [
            jnp.where(is_pos, two_high, jnp.where(is_frc, pltpu.roll(two_high, 3, 1), jnp.where(row8 == 6, t1, t2))),
            jnp.where(is_pos, two_low, jnp.where(is_frc, pltpu.roll(two_low, 3, 1), jnp.where(row8 == 6, t3, 0.0))),
            jnp.where(is_pos, 1.0, zero8),
            zero8,
        ],
        axis=1,
    )
    xtgt[...] = jnp.swapaxes(x_table, 1, 2).astype(bf16)

    def source_side(k):
        src = raw[k]
        at = pl.ds(k * leaves, leaves)
        s_high = rounded(src)
        s_low = rounded(src - s_high)
        s_sum = s_high + s_low
        y1, y2, y3 = split3(pos_sum(s_sum * s_sum))
        pairs = jnp.where(is_pos, s_high, jnp.where(is_frc, pltpu.roll(s_low, 3, 1), 1.0))
        squares = jnp.where(row8 == 0, y1, jnp.where(row8 == 1, y2, jnp.where(row8 == 2, y3, 0.0)))
        yq[at] = jnp.concatenate([pairs, pairs, squares, zero8], axis=1).astype(bf16)
        square = pos_sum(src * src)
        f_at0, f_at6 = pltpu.roll(src, 5, 1), pltpu.roll(src, 3, 1)
        f_dot_y = pos_sum(src * f_at0)
        z = src[:, 2:3, :]
        products = jnp.where(is_pos, f_at0, jnp.where(is_frc, src, f_at6)) * jnp.where(
            is_pos, src[:, 0:1, :], jnp.where(is_frc, src[:, 1:2, :], z)
        )
        second = pltpu.roll(src, 1, 1) * square + pltpu.roll(src, 4, 1) * f_dot_y
        others = jnp.where(
            row8 == 0, f_at6 * z, jnp.where(row8 < 4, pltpu.roll(src, 6, 1), jnp.where(row8 < 7, second, 0.0))
        )
        a, b = split3(products), split3(others)
        feat[at] = jnp.concatenate([a[0], b[0], a[1], b[1], a[2], b[2]], axis=1).astype(bf16)

    source_side(1)

    @pl.when(has_after)
    def _():
        pl.semaphore_wait(ready_sem, 1)
        up.start()

    @pl.when(has_before)
    def _():
        up.wait_recv()

    source_side(0)

    @pl.when(has_after)
    def _():
        down.wait_recv()

    source_side(2)
    small[4].wait()

    def leaf(i, c):
        which = [nbr_ref[n, i] for n in range(nbr_ref.shape[0])]
        q = jnp.dot(xtgt[i], jnp.concatenate([yq[n] for n in which], axis=1), preferred_element_type=f32)
        r = lax.rsqrt(q)
        w = (r * r * r).astype(bf16)
        m = lax.dot_general(
            jnp.concatenate([feat[n] for n in which], axis=1), w, NT_DIMS, preferred_element_type=f32
        )
        moments[i] = m[:16] + m[16:32] + m[32:]
        return c

    lax.fori_loop(0, leaves, leaf, 0, unroll=True)
    m = [moments[:, k, :] for k in range(15)]
    x = [pos_ref[c] for c in range(3)]
    two_e = x[0] * x[0] + x[1] * x[1] + x[2] * x[2] + 2.0 * EPS
    along = x[0] * m[9] + x[1] * m[10] + x[2] * m[11] - (m[0] + m[4] + m[8])
    live = alive[...] * SCALE
    for c in range(3):
        u = two_e * m[9 + c] + x[c] * along + m[12 + c]
        for b in range(3):
            u = u - x[b] * (2.0 * m[3 * b + c] + m[3 * c + b])
        vel_ref[c] = u * live

    def arrivals(first, count, sem):
        part = pl.ds(first, count)
        return pltpu.make_async_remote_copy(
            src_ref=send.at[part], dst_ref=recv.at[part], send_sem=send_sem, recv_sem=sem,
            device_id={"hx": peer(0, 0, 1)}, device_id_type=MESH,
        )

    chips = sorted({(dx, dy) for dx, dy, _ in steps}, key=lambda c: sum(min(d, side - d) for d in c))
    for dx, dy in chips:
        k = dx * side + dy
        own_chip = 1 if k == 0 else 0
        arrivals(2 * k + own_chip, 2 - own_chip, recv_sem.at[k]).wait_recv()
        a, b = recv[2 * k].astype(f32), recv[2 * k + 1].astype(f32)
        gathered[8 * k : 8 * k + 8, :half] = jnp.where(upper, a, pltpu.roll(b, UNIQ, 0)).astype(bf16)
        gathered[8 * k : 8 * k + 8, half:] = jnp.where(upper, pltpu.roll(a, UNIQ, 0), b).astype(bf16)
    small[5].wait()
    for c in ops_copies:
        c.wait()
    arrivals(0, n_hx - 1, recv_sem.at[0]).wait_send()

    @pl.when(has_after)
    def _():
        up.wait_send()

    @pl.when(has_before)
    def _():
        down.wait_send()


def translate_kernel(parts, rows_ref, ops_ref, src_ref, vel_in, out_hbm, vel_hbm, pick, buffer, sems, vel_sem):
    vel_copy = pltpu.make_async_copy(vel_in, vel_hbm, vel_sem)
    vel_copy.start()
    n_dirs, coeffs = ops_ref.shape[:2]
    n_keys = rows_ref.shape[0]
    whose = rows_ref[:, coeffs : coeffs + 2].astype(f32)
    ids = (whose[:, 0:1] * 32.0 + whose[:, 1:2]).astype(jnp.int32)
    for t in range(n_dirs):
        pick[t * n_keys : (t + 1) * n_keys, :] = jnp.where(ids == src_ref[t : t + 1, :], 1.0, 0.0).astype(bf16)

    def product(at, size):
        held = rows_ref[:, :coeffs]
        both = [jnp.dot(held, ops_ref[t, :, at : at + size], preferred_element_type=f32) for t in range(n_dirs)]
        return jnp.concatenate(both, axis=0).T.astype(bf16)

    starts = [sum(parts[:k]) for k in range(len(parts))]
    copies = []
    ready = product(0, parts[0])
    for k, (at, size) in enumerate(zip(starts, parts)):
        later = product(starts[k + 1], parts[k + 1]) if k + 1 < len(parts) else None
        buffer[at : at + size, :] = jnp.dot(ready, pick[...], preferred_element_type=f32).astype(bf16)
        copies.append(pltpu.make_async_copy(buffer.at[pl.ds(at, size)], out_hbm.at[pl.ds(at, size)], sems.at[k]))
        copies[-1].start()
        ready = later
    for c in copies:
        c.wait()
    vel_copy.wait()


def on_device(
    n_hx, n_nb, partial_multipoles, shared_slots, m2l_sources, m2l_ops, positions, forces, leaf_counts, neighbours
):
    rows_t = partial_multipoles[0].T
    coeffs, n_rows = rows_t.shape
    n_dirs, owned = m2l_sources.shape[1:]
    n_near = neighbours.shape[1]
    leaves = leaf_counts.shape[1]
    lanes = positions.shape[2] // leaves
    n_keys = n_hx * UNIQ
    vmem = pl.BlockSpec(memory_space=pltpu.VMEM)
    hbm = pl.BlockSpec(memory_space=pltpu.HBM)
    half = pl.cdiv(coeffs + 8, 256) * 128
    i32 = jnp.int32
    summed, ops, sources, vel = pl.pallas_call(
        functools.partial(exchange_kernel, n_hx, n_nb),
        out_shape=(
            jax.ShapeDtypeStruct((n_keys, 2 * half), bf16),
            jax.ShapeDtypeStruct((n_dirs, coeffs, coeffs), bf16),
            jax.ShapeDtypeStruct((n_dirs, owned), i32),
            jax.ShapeDtypeStruct((3, leaves, lanes), f32),
        ),
        in_specs=[hbm] * 8,
        out_specs=(vmem, vmem, vmem, vmem),
        scratch_shapes=[
            pltpu.VMEM((1, n_rows), i32),
            pltpu.VMEM((3, leaves, lanes), f32),
            pltpu.VMEM((3, leaves, lanes), f32),
            pltpu.SMEM((1, leaves), i32),
            pltpu.SMEM((n_near, leaves), i32),
            pltpu.VMEM((2 * half, n_rows), bf16),
            pltpu.VMEM((n_hx, 2 * UNIQ, half), bf16),
            pltpu.VMEM((n_hx, 2 * UNIQ, half), bf16),
            pltpu.VMEM((3, leaves, 8, lanes), f32),
            pltpu.VMEM((leaves, lanes), f32),
            pltpu.VMEM((3 * leaves, QROWS, lanes), bf16),
            pltpu.VMEM((3 * leaves, FROWS, lanes), bf16),
            pltpu.VMEM((leaves, lanes, QROWS), bf16),
            pltpu.VMEM((leaves, 16, lanes), f32),
            pltpu.SemaphoreType.DMA,
            pltpu.SemaphoreType.DMA((n_hx // 2,)),
            pltpu.SemaphoreType.DMA((2,)),
            pltpu.SemaphoreType.DMA((2,)),
            pltpu.SemaphoreType.REGULAR,
            pltpu.SemaphoreType.REGULAR,
            pltpu.SemaphoreType.REGULAR,
            pltpu.SemaphoreType.DMA((6,)),
            pltpu.SemaphoreType.DMA,
            pltpu.SemaphoreType.DMA((n_dirs,)),
        ],
        compiler_params=pltpu.CompilerParams(
            collective_id=0, has_side_effects=True, vmem_limit_bytes=32 * 1024 * 1024
        ),
        name="exchange",
    )(
        *[
            pltpu.with_memory_space_constraint(v, pltpu.HBM)
            for v in (
                shared_slots, positions.reshape(3, leaves, lanes), forces.reshape(3, leaves, lanes), leaf_counts,
                neighbours[0], m2l_sources[0], rows_t, m2l_ops,
            )
        ]
    )
    parts = [min(256, coeffs - k) for k in range(0, coeffs, 256)]
    out_t, velocity = pl.pallas_call(
        functools.partial(translate_kernel, parts),
        out_shape=(
            jax.ShapeDtypeStruct((coeffs, owned), bf16),
            jax.ShapeDtypeStruct((3, leaves, lanes), f32),
        ),
        in_specs=[vmem] * 4,
        out_specs=(pl.BlockSpec(memory_space=pl.ANY),) * 2,
        scratch_shapes=[
            pltpu.VMEM((n_dirs * n_keys, owned), bf16),
            pltpu.VMEM((coeffs, owned), bf16),
            pltpu.SemaphoreType.DMA((len(parts),)),
            pltpu.SemaphoreType.DMA,
        ],
        compiler_params=pltpu.CompilerParams(vmem_limit_bytes=32 * 1024 * 1024),
        name="translate",
    )(summed, ops, sources, vel)
    return out_t.T[None], velocity.reshape(1, 3, leaves * lanes)


def solution(mesh):
    placed = (
        P("nb", "hx", None),
        P("nb", "hx"),
        P("nb", None, "hx"),
        P(),
        P("nb", None, "hx"),
        P("nb", None, "hx"),
        P("nb", "hx"),
        P("nb", None, "hx"),
    )
    return jax.shard_map(
        functools.partial(on_device, mesh.shape["hx"], mesh.shape["nb"]),
        mesh=mesh,
        in_specs=placed,
        out_specs=(P("nb", "hx", None), P("nb", None, "hx")),
        check_vma=False,
    )
```

```python
import functools
import math

import jax
import jax.numpy as jnp
from jax import lax
from jax.experimental import pallas as pl
from jax.experimental.pallas import tpu as pltpu
from jax.sharding import PartitionSpec as P

EPS = 0.01
SCALE = 1.0 / (8.0 * math.pi)
MESH = pl.DeviceIdType.MESH
UNIQ = 4
CAP = 16
QROWS = 32
FROWS = 48
f32 = jnp.float32
bf16 = jnp.bfloat16
NT_DIMS = (((1,), (1,)), ((), ()))


def peer_steps(n_hx):
    side = math.isqrt(n_hx // 2)
    steps = [(dx, dy, dc) for dx in range(side) for dy in range(side) for dc in range(2) if dx or dy or dc]
    return side, sorted(steps, key=lambda s: -(min(s[0], side - s[0]) + min(s[1], side - s[1])))


def rounded(v):
    return v.astype(bf16).astype(f32)


def split3(v):
    a = rounded(v)
    b = rounded(v - a)
    return a, b, rounded(v - a - b)


def rank_keys(slots):
    lane = lax.broadcasted_iota(jnp.int32, slots.shape, 1)
    group = lax.broadcasted_iota(jnp.int32, slots.shape, 0)
    place = lane & (CAP - 1)
    dup = jnp.zeros(slots.shape, jnp.int32)
    for s in range(1, CAP):
        same = (pltpu.roll(slots, s, 1) == slots) & (place >= s)
        dup = jnp.where(same, 1, dup)
    first = (dup == 0) & (slots >= 0)
    named = jnp.where(first, slots, 1 << 20)
    rank = jnp.zeros(slots.shape, jnp.int32)
    for s in range(1, CAP):
        below = (pltpu.roll(named, s, 1) < slots) & (place >= s)
        rank = rank + jnp.where(below, 1, 0)
        below = (pltpu.roll(named, 128 - s, 1) < slots) & (place < CAP - s)
        rank = rank + jnp.where(below, 1, 0)
    key = jnp.where(slots >= 0, group * (128 // CAP * UNIQ) + (lane >> 4) * UNIQ + rank, -1)
    return key, first


def exchange_kernel(
    n_hx, n_nb, slots_hbm, pos_hbm, frc_hbm, counts_hbm, nbr_hbm, src_hbm, rows_hbm, ops_hbm,
    gathered, ops, src_ref, vel_ref,
    slots_ref, pos_ref, frc_ref, counts_ref, nbr_ref,
    rows, send, recv, raw, alive, yq, feat, xtgt, moments,
    send_sem, recv_sem, halo_send, halo_recv, ready_sem, news_sem, all_sem, small_sem, rows_sem, ops_sem,
):
    hx, nb = lax.axis_index("hx"), lax.axis_index("nb")
    after, before = lax.min(nb + 1, n_nb - 1), lax.max(nb - 1, 0)
    has_after, has_before = nb < n_nb - 1, nb > 0
    coeffs = rows_hbm.shape[0]
    leaves, lanes = pos_ref.shape[1], pos_ref.shape[2]
    half = send.shape[2]
    n_keys = n_hx * UNIQ

    small = [
        pltpu.make_async_copy(a, b, small_sem.at[k])
        for k, (a, b) in enumerate(
            (
                (slots_hbm, slots_ref), (counts_hbm, counts_ref), (pos_hbm, pos_ref), (frc_hbm, frc_ref),
                (nbr_hbm, nbr_ref), (src_hbm, src_ref),
            )
        )
    ]
    for c in small[:4]:
        c.start()
    rows_copy = pltpu.make_async_copy(rows_hbm, rows.at[pl.ds(0, coeffs), :], rows_sem)
    rows_copy.start()
    for c in small[4:]:
        c.start()

    side, steps = peer_steps(n_hx)
    at_x, at_y, at_c = hx // (2 * side), lax.rem(hx // 2, side), lax.rem(hx, 2)

    def peer(dx, dy, dc):
        return lax.rem(at_x + dx, side) * (2 * side) + lax.rem(at_y + dy, side) * 2 + lax.rem(at_c + dc, 2)

    barrier = pltpu.get_barrier_semaphore()
    partner = peer(0, 0, 1)
    second = at_c == 1

    for dx, dy in sorted({(dx, dy) for dx, dy, _ in steps} - {(0, 0)}, key=lambda c: -sum(min(d, side - d) for d in c)):
        pl.semaphore_signal(barrier, inc=1, device_id={"hx": peer(dx, dy, 1 - at_c)}, device_id_type=MESH)
    pl.semaphore_signal(barrier, inc=1, device_id={"hx": partner}, device_id_type=MESH)

    @pl.when(has_after)
    def _():
        pl.semaphore_signal(barrier, inc=1, device_id={"hx": hx - at_c, "nb": after}, device_id_type=MESH)

    ops_copies = [pltpu.make_async_copy(ops_hbm.at[t], ops.at[t], ops_sem.at[t]) for t in range(ops.shape[0])]

    for c in small[1:4]:
        c.wait()
    lane_ids = lax.broadcasted_iota(jnp.int32, (1, lanes), 1)
    for l in range(leaves):
        live = jnp.where(lane_ids < counts_ref[0, l], 1.0, 0.0).astype(f32)
        alive[l : l + 1, :] = live
        block = [pos_ref[c, l : l + 1, :] for c in range(3)]
        block += [frc_ref[c, l : l + 1, :] * live for c in range(3)]
        block += [jnp.ones((1, lanes), f32), jnp.zeros((1, lanes), f32)]
        raw[1, l] = jnp.concatenate(block, axis=0)

    edge = jnp.zeros((leaves, 8, lanes), f32)

    @pl.when(nb == 0)
    def _():
        raw[0] = edge

    @pl.when(nb == n_nb - 1)
    def _():
        raw[2] = edge

    def halo(k, target):
        return pltpu.make_async_remote_copy(
            src_ref=raw.at[1], dst_ref=raw.at[k], send_sem=halo_send.at[k // 2], recv_sem=halo_recv.at[k // 2],
            device_id={"nb": target}, device_id_type=MESH,
        )

    up, down = halo(0, after), halo(2, before)

    @pl.when(jnp.logical_not(second))
    def _():
        pl.semaphore_wait(barrier, 1 + 2 * lax.min(nb, 1))

        @pl.when(has_before)
        def _():
            pl.semaphore_signal(news_sem, inc=1, device_id={"hx": partner}, device_id_type=MESH)

    @pl.when(has_before)
    def _():
        @pl.when(second)
        def _():
            pl.semaphore_wait(news_sem, 1)

        down.start()
        pl.semaphore_signal(ready_sem, inc=1, device_id={"nb": before}, device_id_type=MESH)

    small[0].wait()
    slots = slots_ref[...]
    four = [slots[:, g * lanes : (g + 1) * lanes] for g in range(4)]
    slots8 = jnp.concatenate(four + four, axis=0)
    key, first = rank_keys(slots8)
    key_ids = lax.broadcasted_iota(jnp.int32, (n_keys, lanes), 0)
    choose = jnp.concatenate(
        [jnp.where(key_ids == key[g : g + 1, :], 1.0, 0.0).astype(bf16) for g in range(4)], axis=1
    )
    high = jnp.where(first, slots8 >> 5, 0).astype(f32)
    low = jnp.where(first, slots8 & 31, 0).astype(f32)
    zero6 = jnp.zeros((6, lanes), f32)
    marks = jnp.concatenate(
        [jnp.concatenate([high[g : g + 1], low[g : g + 1], zero6], axis=0) for g in range(4)], axis=1
    )
    rows[coeffs : coeffs + 8, :] = marks.astype(bf16)
    rows[coeffs + 8 :, :] = jnp.zeros((rows.shape[0] - coeffs - 8, rows.shape[1]), bf16)

    rows_copy.wait()
    sums = lax.dot_general(choose, rows[...], NT_DIMS, preferred_element_type=f32)
    upper = lax.broadcasted_iota(jnp.int32, (8, half), 0) < UNIQ
    for v in range(n_hx // 2):
        left, right = sums[8 * v : 8 * v + 8, :half], sums[8 * v : 8 * v + 8, half:]
        send[2 * v] = jnp.where(upper, left, pltpu.roll(right, UNIQ, 0)).astype(bf16)
        send[2 * v + 1] = jnp.where(upper, pltpu.roll(left, UNIQ, 0), right).astype(bf16)

    @pl.when(second)
    def _():
        pl.semaphore_wait(barrier, n_hx - 1)
        pl.semaphore_signal(all_sem, inc=1, device_id={"hx": partner}, device_id_type=MESH)

    @pl.when(jnp.logical_not(second))
    def _():
        pl.semaphore_wait(all_sem, 1)

    def chunk(step):
        place = (step[0] * side + step[1]) * 2 + step[2]
        target = peer(*step)
        return pltpu.make_async_remote_copy(
            src_ref=send.at[target], dst_ref=recv.at[place], send_sem=send_sem, recv_sem=recv_sem.at[place // 2],
            device_id={"hx": target}, device_id_type=MESH,
        )

    for step in steps:
        chunk(step).start()
    recv[0] = send[hx]
    for c in ops_copies:
        c.start()

    row8 = lax.broadcasted_iota(jnp.int32, (leaves, 8, lanes), 1)
    zero8 = jnp.zeros((leaves, 8, lanes), f32)
    is_pos, is_frc = row8 < 3, (row8 >= 3) & (row8 < 6)

    def pos_sum(v):
        return jnp.sum(jnp.where(is_pos, v, 0.0), axis=1, keepdims=True)

    own = raw[1]
    own_high = rounded(own)
    own_low = rounded(own - own_high)
    x_sum = own_high + own_low
    t1, t2, t3 = split3(pos_sum(x_sum * x_sum) + EPS)
    two_high, two_low = -2.0 * own_high, -2.0 * own_low
    x_table = jnp.concatenate(
        [
            jnp.where(is_pos, two_high, jnp.where(is_frc, pltpu.roll(two_high, 3, 1), jnp.where(row8 == 6, t1, t2))),
            jnp.where(is_pos, two_low, jnp.where(is_frc, pltpu.roll(two_low, 3, 1), jnp.where(row8 == 6, t3, 0.0))),
            jnp.where(is_pos, 1.0, zero8),
            zero8,
        ],
        axis=1,
    )
    xtgt[...] = jnp.swapaxes(x_table, 1, 2).astype(bf16)

    def source_side(k):
        src = raw[k]
        at = pl.ds(k * leaves, leaves)
        s_high = rounded(src)
        s_low = rounded(src - s_high)
        s_sum = s_high + s_low
        y1, y2, y3 = split3(pos_sum(s_sum * s_sum))
        pairs = jnp.where(is_pos, s_high, jnp.where(is_frc, pltpu.roll(s_low, 3, 1), 1.0))
        squares = jnp.where(row8 == 0, y1, jnp.where(row8 == 1, y2, jnp.where(row8 == 2, y3, 0.0)))
        yq[at] = jnp.concatenate([pairs, pairs, squares, zero8], axis=1).astype(bf16)
        square = pos_sum(src * src)
        f_at0, f_at6 = pltpu.roll(src, 5, 1), pltpu.roll(src, 3, 1)
        f_dot_y = pos_sum(src * f_at0)
        z = src[:, 2:3, :]
        products = jnp.where(is_pos, f_at0, jnp.where(is_frc, src, f_at6)) * jnp.where(
            is_pos, src[:, 0:1, :], jnp.where(is_frc, src[:, 1:2, :], z)
        )
        second = pltpu.roll(src, 1, 1) * square + pltpu.roll(src, 4, 1) * f_dot_y
        others = jnp.where(
            row8 == 0, f_at6 * z, jnp.where(row8 < 4, pltpu.roll(src, 6, 1), jnp.where(row8 < 7, second, 0.0))
        )
        a, b = split3(products), split3(others)
        feat[at] = jnp.concatenate([a[0], b[0], a[1], b[1], a[2], b[2]], axis=1).astype(bf16)

    source_side(1)

    @pl.when(has_after)
    def _():
        pl.semaphore_wait(ready_sem, 1)
        up.start()

    @pl.when(has_before)
    def _():
        up.wait_recv()

    source_side(0)

    @pl.when(has_after)
    def _():
        down.wait_recv()

    source_side(2)
    small[4].wait()

    def leaf(i, c):
        which = [nbr_ref[n, i] for n in range(nbr_ref.shape[0])]
        q = jnp.dot(xtgt[i], jnp.concatenate([yq[n] for n in which], axis=1), preferred_element_type=f32)
        r = lax.rsqrt(q)
        w = (r * r * r).astype(bf16)
        m = lax.dot_general(
            jnp.concatenate([feat[n] for n in which], axis=1), w, NT_DIMS, preferred_element_type=f32
        )
        moments[i] = m[:16] + m[16:32] + m[32:]
        return c

    lax.fori_loop(0, leaves, leaf, 0, unroll=True)
    m = [moments[:, k, :] for k in range(15)]
    x = [pos_ref[c] for c in range(3)]
    two_e = x[0] * x[0] + x[1] * x[1] + x[2] * x[2] + 2.0 * EPS
    along = x[0] * m[9] + x[1] * m[10] + x[2] * m[11] - (m[0] + m[4] + m[8])
    live = alive[...] * SCALE
    for c in range(3):
        u = two_e * m[9 + c] + x[c] * along + m[12 + c]
        for b in range(3):
            u = u - x[b] * (2.0 * m[3 * b + c] + m[3 * c + b])
        vel_ref[c] = u * live

    def arrivals(first, count, sem):
        part = pl.ds(first, count)
        return pltpu.make_async_remote_copy(
            src_ref=send.at[part], dst_ref=recv.at[part], send_sem=send_sem, recv_sem=sem,
            device_id={"hx": peer(0, 0, 1)}, device_id_type=MESH,
        )

    chips = sorted({(dx, dy) for dx, dy, _ in steps}, key=lambda c: -sum(min(d, side - d) for d in c))
    for dx, dy in chips:
        k = dx * side + dy
        own_chip = 1 if k == 0 else 0
        arrivals(2 * k + own_chip, 2 - own_chip, recv_sem.at[k]).wait_recv()
        a, b = recv[2 * k].astype(f32), recv[2 * k + 1].astype(f32)
        gathered[8 * k : 8 * k + 8, :half] = jnp.where(upper, a, pltpu.roll(b, UNIQ, 0)).astype(bf16)
        gathered[8 * k : 8 * k + 8, half:] = jnp.where(upper, pltpu.roll(a, UNIQ, 0), b).astype(bf16)
    small[5].wait()
    for c in ops_copies:
        c.wait()
    arrivals(0, n_hx - 1, recv_sem.at[0]).wait_send()

    @pl.when(has_after)
    def _():
        up.wait_send()

    @pl.when(has_before)
    def _():
        down.wait_send()


def translate_kernel(parts, rows_ref, ops_ref, src_ref, vel_in, out_hbm, vel_hbm, pick, buffer, sems, vel_sem):
    vel_copy = pltpu.make_async_copy(vel_in, vel_hbm, vel_sem)
    vel_copy.start()
    n_dirs, coeffs = ops_ref.shape[:2]
    n_keys = rows_ref.shape[0]
    whose = rows_ref[:, coeffs : coeffs + 2].astype(f32)
    ids = (whose[:, 0:1] * 32.0 + whose[:, 1:2]).astype(jnp.int32)
    for t in range(n_dirs):
        pick[t * n_keys : (t + 1) * n_keys, :] = jnp.where(ids == src_ref[t : t + 1, :], 1.0, 0.0).astype(bf16)

    def product(at, size):
        held = rows_ref[:, :coeffs]
        both = [jnp.dot(held, ops_ref[t, :, at : at + size], preferred_element_type=f32) for t in range(n_dirs)]
        return jnp.concatenate(both, axis=0).T.astype(bf16)

    starts = [sum(parts[:k]) for k in range(len(parts))]
    copies = []
    ready = product(0, parts[0])
    for k, (at, size) in enumerate(zip(starts, parts)):
        later = product(starts[k + 1], parts[k + 1]) if k + 1 < len(parts) else None
        buffer[at : at + size, :] = jnp.dot(ready, pick[...], preferred_element_type=f32).astype(bf16)
        copies.append(pltpu.make_async_copy(buffer.at[pl.ds(at, size)], out_hbm.at[pl.ds(at, size)], sems.at[k]))
        copies[-1].start()
        ready = later
    for c in copies:
        c.wait()
    vel_copy.wait()


def on_device(
    n_hx, n_nb, partial_multipoles, shared_slots, m2l_sources, m2l_ops, positions, forces, leaf_counts, neighbours
):
    rows_t = partial_multipoles[0].T
    coeffs, n_rows = rows_t.shape
    n_dirs, owned = m2l_sources.shape[1:]
    n_near = neighbours.shape[1]
    leaves = leaf_counts.shape[1]
    lanes = positions.shape[2] // leaves
    n_keys = n_hx * UNIQ
    vmem = pl.BlockSpec(memory_space=pltpu.VMEM)
    hbm = pl.BlockSpec(memory_space=pltpu.HBM)
    half = pl.cdiv(coeffs + 8, 256) * 128
    i32 = jnp.int32
    summed, ops, sources, vel = pl.pallas_call(
        functools.partial(exchange_kernel, n_hx, n_nb),
        out_shape=(
            jax.ShapeDtypeStruct((n_keys, 2 * half), bf16),
            jax.ShapeDtypeStruct((n_dirs, coeffs, coeffs), bf16),
            jax.ShapeDtypeStruct((n_dirs, owned), i32),
            jax.ShapeDtypeStruct((3, leaves, lanes), f32),
        ),
        in_specs=[hbm] * 8,
        out_specs=(vmem, vmem, vmem, vmem),
        scratch_shapes=[
            pltpu.VMEM((1, n_rows), i32),
            pltpu.VMEM((3, leaves, lanes), f32),
            pltpu.VMEM((3, leaves, lanes), f32),
            pltpu.SMEM((1, leaves), i32),
            pltpu.SMEM((n_near, leaves), i32),
            pltpu.VMEM((2 * half, n_rows), bf16),
            pltpu.VMEM((n_hx, 2 * UNIQ, half), bf16),
            pltpu.VMEM((n_hx, 2 * UNIQ, half), bf16),
            pltpu.VMEM((3, leaves, 8, lanes), f32),
            pltpu.VMEM((leaves, lanes), f32),
            pltpu.VMEM((3 * leaves, QROWS, lanes), bf16),
            pltpu.VMEM((3 * leaves, FROWS, lanes), bf16),
            pltpu.VMEM((leaves, lanes, QROWS), bf16),
            pltpu.VMEM((leaves, 16, lanes), f32),
            pltpu.SemaphoreType.DMA,
            pltpu.SemaphoreType.DMA((n_hx // 2,)),
            pltpu.SemaphoreType.DMA((2,)),
            pltpu.SemaphoreType.DMA((2,)),
            pltpu.SemaphoreType.REGULAR,
            pltpu.SemaphoreType.REGULAR,
            pltpu.SemaphoreType.REGULAR,
            pltpu.SemaphoreType.DMA((6,)),
            pltpu.SemaphoreType.DMA,
            pltpu.SemaphoreType.DMA((n_dirs,)),
        ],
        compiler_params=pltpu.CompilerParams(
            collective_id=0, has_side_effects=True, vmem_limit_bytes=32 * 1024 * 1024
        ),
        name="exchange",
    )(
        *[
            pltpu.with_memory_space_constraint(v, pltpu.HBM)
            for v in (
                shared_slots, positions.reshape(3, leaves, lanes), forces.reshape(3, leaves, lanes), leaf_counts,
                neighbours[0], m2l_sources[0], rows_t, m2l_ops,
            )
        ]
    )
    parts = [min(256, coeffs - k) for k in range(0, coeffs, 256)]
    out_t, velocity = pl.pallas_call(
        functools.partial(translate_kernel, parts),
        out_shape=(
            jax.ShapeDtypeStruct((coeffs, owned), bf16),
            jax.ShapeDtypeStruct((3, leaves, lanes), f32),
        ),
        in_specs=[vmem] * 4,
        out_specs=(pl.BlockSpec(memory_space=pl.ANY),) * 2,
        scratch_shapes=[
            pltpu.VMEM((n_dirs * n_keys, owned), bf16),
            pltpu.VMEM((coeffs, owned), bf16),
            pltpu.SemaphoreType.DMA((len(parts),)),
            pltpu.SemaphoreType.DMA,
        ],
        compiler_params=pltpu.CompilerParams(vmem_limit_bytes=32 * 1024 * 1024),
        name="translate",
    )(summed, ops, sources, vel)
    return out_t.T[None], velocity.reshape(1, 3, leaves * lanes)


def solution(mesh):
    placed = (
        P("nb", "hx", None),
        P("nb", "hx"),
        P("nb", None, "hx"),
        P(),
        P("nb", None, "hx"),
        P("nb", None, "hx"),
        P("nb", "hx"),
        P("nb", None, "hx"),
    )
    return jax.shard_map(
        functools.partial(on_device, mesh.shape["hx"], mesh.shape["nb"]),
        mesh=mesh,
        in_specs=placed,
        out_specs=(P("nb", "hx", None), P("nb", None, "hx")),
        check_vma=False,
    )
```
